32 devices in a mesh: grp: 4 (over x, core), blk: 8 (over z, y).
Axes of the slice: x: 2, y: 2, z: 4, core: 2. Of those that a mesh axis runs over, the one named last changes fastest.
Arguments:
- vector: bfloat16 [32, 128], P(('grp', 'blk')), may hold values from -6 to 6
- integrals: bfloat16 [1024, 500, 500], P(('grp', 'blk')), may hold values from -0.072 to 0.072
- orbitals: bfloat16 [26, 500], replicated, may hold values from -0.25 to 0.25
- alpha_addr: int32 [32, 676], replicated, may hold values from 0 to 31
- alpha_sign: int32 [32, 676], replicated, may hold values from -1 to 1
- beta_addr: int32 [128, 676], replicated, may hold values from 0 to 127
- beta_sign: int32 [128, 676], replicated, may hold values from -1 to 1
- seg_alpha: int32 [32], replicated, may hold values from 0 to 9, never falling along the last dimension, each value on 1 to 6 neighbouring positions
- seg_beta: int32 [128], replicated, may hold values from 0 to 9, never falling along the last dimension, each value on 1 to 25 neighbouring positions
- allowed: int32 [10, 10], replicated, may hold values 0 or 1
Outputs:
- sigma_t: float32 [128, 32], P(('grp', 'blk'))
The draws below stay inside these ranges and needn't reach their ends.
All inputs are finite; a program needn't handle non-finite values.
Results may differ from the reference program's by a relative error of at most 0.0056.
Values may be sent and summed in bfloat16 or wider, within the bound.
No kernel may reach another device: no remote copies, remote signals or barrier semaphores. Data moves between devices by JAX's collectives and lax.ppermute only.
A program may use at most 64 MiB of HBM per device.

```python
import math
import jax
import jax.numpy as jnp
import numpy as np
from jax import lax

NORB = 26
NPAIR = 676
NBAS = 500
NAUX = 1024
NBLK = 10
B_DEV = 4
NA = 32
NB = 128


def draw_integrals(key, part):
    levels = jnp.arange(NAUX, dtype=jnp.float32) / NAUX
    scales = (0.003 * jnp.power(4.0, levels))[:, None, None]
    values = jnp.clip(jax.random.normal(key, (NAUX, NBAS, NBAS), jnp.float32), -6.0, 6.0)
    return (values * scales).astype(jnp.bfloat16)


def with_ends(values, key, low, high):
    place = [jax.random.randint(jax.random.fold_in(key, axis), (), 0, length) for axis, length in enumerate(values.shape)]
    main_axis = values.shape.index(max(values.shape))
    next_to = place[:main_axis] + [(place[main_axis] + 1) % values.shape[main_axis]] + place[main_axis + 1:]
    return values.at[tuple(place)].set(low).at[tuple(next_to)].set(high)


def shard_levels(rng, extent, split, least, high):
    loudness = 1.0
    for position, shards_of in split:
        heights = jax.random.uniform(jax.random.fold_in(jax.random.fold_in(rng, 6), position), (shards_of,), jnp.float32, least / len(split), high / len(split))
        loudness = loudness * jnp.repeat(jnp.exp(heights), extent[position] // shards_of).reshape((-1,) + (1,) * (len(extent) - 1 - position))
    return loudness


def split_up(amount, total, bound, skew):
    weights = [(1 << 20) // math.isqrt(standing ** skew) + 1 for standing in range(2, amount + 1)]
    surplus, given = total - bound - (amount - 1), [1] * (amount - 1)
    while surplus > 0:
        candidates = [i for i in range(amount - 1) if given[i] < bound]
        pool, budget = sum([weights[i] for i in candidates]), surplus
        for i in candidates:
            more = min(bound - given[i], max(1, budget * weights[i] // pool), surplus)
            given[i] = given[i] + more
            surplus = surplus - more
    return np.array([bound] + given)


def ragged(key, count, total, limit, lean):
    if count == 2:
        one = jax.random.randint(key, (), max(1, total - limit), min(limit, total - 1) + 1)
        return jnp.stack([one, total - one])
    lengths = jnp.asarray(split_up(count, total, limit, lean), jnp.int32)
    pairs = (count - 1) // 2
    giver, receiver = lengths[1:1 + 2 * pairs:2], lengths[2:2 + 2 * pairs:2]
    margin = jnp.minimum(giver - 1, limit - receiver)
    moved = jax.random.randint(jax.random.fold_in(key, 1), (pairs,), 0, 1 << 20) % (margin + 1)
    lengths = lengths.at[1:1 + 2 * pairs:2].set(giver - moved).at[2:2 + 2 * pairs:2].set(receiver + moved)
    return lengths[jax.random.permutation(jax.random.fold_in(key, 2), count)]


def normal_values(stream_key, shape, scale, reach, shards=(), kind=jnp.bfloat16):
    entries = jax.random.normal(stream_key, shape, jnp.float32) * scale
    if len(shards) > 0:
        entries = shard_levels(stream_key, shape, shards, -0.22, 0.18) * entries
    return jnp.clip(entries, min=-reach, max=reach).astype(kind)


def setup_inputs(seed: int = 0) -> dict:
    key_list = jax.random.split(jax.random.key(seed), 11)
    vector = normal_values(key_list[0], (NA, NB), 1.0, 6.0, ((0, 32),))
    integrals = draw_integrals(jax.random.fold_in(key_list[10], 71), 0)
    orbitals = normal_values(key_list[2], (NORB, NBAS), NBAS ** -0.5, 0.25)
    alpha_addr = with_ends(jax.random.randint(key_list[3], (NA, NPAIR), 0, NA), jax.random.fold_in(key_list[3], 1), 0, NA - 1).astype(jnp.int32)
    alpha_sign = with_ends(jax.random.randint(key_list[4], (NA, NPAIR), -1, 2), jax.random.fold_in(key_list[4], 1), -1, 1).astype(jnp.int32)
    beta_addr = with_ends(jax.random.randint(key_list[5], (NB, NPAIR), 0, NB), jax.random.fold_in(key_list[5], 1), 0, NB - 1).astype(jnp.int32)
    beta_sign = with_ends(jax.random.randint(key_list[6], (NB, NPAIR), -1, 2), jax.random.fold_in(key_list[6], 1), -1, 1).astype(jnp.int32)
    seg_alpha = jnp.searchsorted(jnp.cumsum(ragged(key_list[7], NBLK, NA, 2 * NA // NBLK, 2)), jnp.arange(NA), side="right").astype(jnp.int32)
    seg_beta = jnp.searchsorted(jnp.cumsum(ragged(key_list[8], NBLK, NB, 2 * NB // NBLK, 2)), jnp.arange(NB), side="right").astype(jnp.int32)
    allowed = with_ends((jax.random.randint(key_list[9], (NBLK, NBLK), 0, 4) < 3).astype(jnp.int32), jax.random.fold_in(key_list[9], 1), 0, 1)
    return dict(vector=vector, integrals=integrals, orbitals=orbitals, alpha_addr=alpha_addr, alpha_sign=alpha_sign, beta_addr=beta_addr, beta_sign=beta_sign, seg_alpha=seg_alpha, seg_beta=seg_beta, allowed=allowed)


def onehot(segment_ids):
    return (segment_ids[:, None] == jnp.arange(NBLK, dtype=jnp.int32)[None, :]).astype(jnp.float32)


def reference(vector, integrals, orbitals, alpha_addr, alpha_sign, beta_addr, beta_sign, seg_alpha, seg_beta, allowed):
    allowed_f = allowed.astype(jnp.float32)
    det_mask = jnp.dot(jnp.dot(onehot(seg_alpha), allowed_f, precision=lax.Precision.HIGHEST), onehot(seg_beta).T, precision=lax.Precision.HIGHEST)
    masked = (vector.astype(jnp.float32) * det_mask).astype(jnp.bfloat16)
    orbital_f = orbitals.astype(jnp.float32)

    def transform(slab):
        half_done = jnp.einsum('jn,pmn->pjm', orbital_f, slab.astype(jnp.float32)).astype(jnp.bfloat16)
        return jnp.einsum('im,pjm->pij', orbital_f, half_done.astype(jnp.float32)).astype(jnp.bfloat16)

    factors = lax.map(transform, integrals.reshape(-1, 8, NBAS, NBAS)).reshape(NAUX, NPAIR)
    factor_f = factors.astype(jnp.float32)
    coulomb = jnp.dot(factor_f.T, factor_f, precision=lax.Precision.HIGHEST).astype(jnp.bfloat16)
    coulomb_f = coulomb.astype(jnp.float32)
    beta_local = jnp.arange(B_DEV, dtype=jnp.int32)
    pair_ids = jnp.arange(NPAIR, dtype=jnp.int32)
    sign_alpha = alpha_sign.astype(jnp.float32)

    def beta_block(tables):
        block_addr, block_sign = tables
        pair_terms = jnp.take(masked, block_addr, axis=1) * block_sign.astype(jnp.bfloat16)[None]
        products = jnp.dot(pair_terms.reshape(-1, NPAIR).astype(jnp.float32), coulomb_f.T, precision=lax.Precision.HIGHEST)
        flattened = products.astype(jnp.bfloat16).reshape(-1)
        gather_index = alpha_addr[None, :, :] * (B_DEV * NPAIR) + beta_local[:, None, None] * NPAIR + pair_ids[None, None, :]
        picked = jnp.take(flattened, gather_index).astype(jnp.float32)
        return jnp.sum(picked * sign_alpha[None], axis=2)

    sigma_all = lax.map(beta_block, (beta_addr.reshape(-1, B_DEV, NPAIR), beta_sign.reshape(-1, B_DEV, NPAIR)))
    return sigma_all.reshape(NB, NA) * det_mask.T
```

```python
import functools

import jax
import jax.numpy as jnp
from jax import lax
from jax.experimental import pallas as pl
from jax.experimental.pallas import tpu as pltpu
from jax.sharding import PartitionSpec as P

AXES = ("grp", "blk")
LANES = 128
SUBLANES = 8
PACK = 16
NT = (((1,), (1,)), ((), ()))


def transform_kernel(low_ref, high_ref, orb_ref, out_ref, half_ref, turn_ref, flat_ref, *, rows, half, stride):
    norb = orb_ref.shape[0]
    groups = low_ref.shape[1] // PACK
    step = pl.program_id(0)
    weights = orb_ref[...]
    total = None
    for side, block_ref in enumerate((low_ref, high_ref)):
        for group in range(groups):
            place = (side * groups + group) * 32
            pieces = []
            if place:
                pieces.append(jnp.zeros((place, weights.shape[1]), jnp.bfloat16))
            pieces.append(weights)
            pieces.append(jnp.zeros((LANES - place - norb, weights.shape[1]), jnp.bfloat16))
            placed = jnp.concatenate(pieces, axis=0)
            block = block_ref[:, group * PACK : (group + 1) * PACK, :].reshape(rows * PACK, block_ref.shape[2])
            part = lax.dot_general(block, placed, NT, preferred_element_type=jnp.float32)
            total = part if total is None else total + part
    for row in range(rows):
        half_ref[pl.ds(step * rows + row, PACK, stride=stride), :] = total[row * PACK : (row + 1) * PACK, :]

    @pl.when(step == pl.num_programs(0) - 1)
    def _():
        first = weights[:, :half]
        second = weights[:, half : 2 * half]
        for r in range(PACK):
            right = half_ref[r * stride : r * stride + half, :].astype(jnp.bfloat16)
            a = jnp.dot(first, right, preferred_element_type=jnp.float32)
            b = jnp.dot(second, right, preferred_element_type=jnp.float32)
            turn_ref[pl.ds(r, norb, stride=PACK), :] = a + pltpu.roll(b, LANES - groups * 32, 1)
        for i in range(norb):
            piece = turn_ref[i * PACK : (i + 1) * PACK, :]
            for group in range(groups):
                flat_ref[group * PACK : (group + 1) * PACK, i * norb : (i + 1) * norb] = piece[
                    :, group * 32 : group * 32 + norb
                ]
        out_ref[...] = flat_ref[...].astype(jnp.bfloat16)


def transform(integrals, orbitals):
    aux, nbas, _ = integrals.shape
    norb = orbitals.shape[0]
    half = nbas // 2
    if aux % PACK or (aux // PACK) * 64 != LANES or norb > 32 or nbas % 2:
        half_done = jnp.einsum("jn,pmn->pjm", orbitals, integrals, preferred_element_type=jnp.float32).astype(
            jnp.bfloat16
        )
        return (
            jnp.einsum("im,pjm->pij", orbitals, half_done, preferred_element_type=jnp.float32)
            .reshape(aux, norb * norb)
            .astype(jnp.bfloat16)
        )
    rows = max(r for r in range(1, 33) if half % r == 0)
    steps = half // rows
    stride = -(-half // SUBLANES) * SUBLANES
    turned = jnp.transpose(integrals, (1, 0, 2))
    return pl.pallas_call(
        functools.partial(transform_kernel, rows=rows, half=half, stride=stride),
        grid=(steps,),
        in_specs=[
            pl.BlockSpec((rows, aux, nbas), lambda s: (s, 0, 0)),
            pl.BlockSpec((rows, aux, nbas), lambda s, steps=steps: (s + steps, 0, 0)),
            pl.BlockSpec((norb, nbas), lambda s: (0, 0)),
        ],
        out_specs=pl.BlockSpec((aux, norb * norb), lambda s: (0, 0)),
        out_shape=jax.ShapeDtypeStruct((aux, norb * norb), jnp.bfloat16),
        scratch_shapes=[
            pltpu.VMEM((PACK * stride, LANES), jnp.float32),
            pltpu.VMEM((norb * PACK, LANES), jnp.float32),
            pltpu.VMEM((aux, norb * norb), jnp.float32),
        ],
        compiler_params=pltpu.CompilerParams(
            dimension_semantics=("arbitrary",), vmem_limit_bytes=40 * 1024 * 1024
        ),
        name="transform",
    )(turned, turned, orbitals)


def alpha_kernel(f_ref, addr_ref, sign_ref, seg_a_ref, seg_b_ref, allowed_ref, h_ref, mask_ref):
    aux, pairs = f_ref.shape
    n_alpha = addr_ref.shape[0]
    blocks = allowed_ref.shape[0]
    side = LANES // aux
    factors = f_ref[...]
    addr = addr_ref[...]
    sign = sign_ref[...].astype(jnp.float32)
    total = None
    for q in range(side):
        hot = [jnp.where(addr == g * side + q, sign, 0.0) for g in range(n_alpha // side)]
        left = jnp.concatenate(hot, axis=0).astype(jnp.bfloat16)
        pieces = []
        if q:
            pieces.append(jnp.zeros((q * aux, pairs), jnp.bfloat16))
        pieces.append(factors)
        if q + 1 < side:
            pieces.append(jnp.zeros((LANES - (q + 1) * aux, pairs), jnp.bfloat16))
        part = lax.dot_general(left, jnp.concatenate(pieces, axis=0), NT, preferred_element_type=jnp.float32)
        total = part if total is None else total + part
    for g in range(n_alpha // side):
        h_ref[:, g * LANES : (g + 1) * LANES] = total[g * n_alpha : (g + 1) * n_alpha, :]
    hot_b = (
        lax.broadcasted_iota(jnp.int32, (blocks, seg_b_ref.shape[1]), 0) == seg_b_ref[...]
    ).astype(jnp.float32)
    hot_a = (lax.broadcasted_iota(jnp.int32, (blocks, n_alpha), 0) == seg_a_ref[...]).astype(jnp.float32)
    columns = jnp.dot(allowed_ref[...].astype(jnp.float32), hot_b, preferred_element_type=jnp.float32)
    mask_ref[...] = lax.dot_general(
        hot_a, columns, (((0,), (0,)), ((), ())), preferred_element_type=jnp.float32
    )


def alpha_side(factors, alpha_addr, alpha_sign, seg_alpha, seg_beta, allowed):
    n_alpha = alpha_addr.shape[0]
    n_beta = seg_beta.shape[0]
    return pl.pallas_call(
        alpha_kernel,
        out_shape=(
            jax.ShapeDtypeStruct((n_alpha, n_alpha * factors.shape[0]), jnp.float32),
            jax.ShapeDtypeStruct((n_alpha, n_beta), jnp.float32),
        ),
        name="alpha_side",
    )(factors, alpha_addr, alpha_sign, seg_alpha.reshape(1, -1), seg_beta.reshape(1, -1), allowed)


def beta_kernel(vec_ref, f_ref, h_ref, mask_ref, addr_ref, sign_ref, out_ref, source_ref, pairs_ref, t_ref, turn_ref):
    aux, pairs = f_ref.shape
    n_alpha, n_beta = mask_ref.shape
    held, padded, _ = pairs_ref.shape
    chunks = n_beta // LANES
    turns = n_alpha // held
    source_ref[...] = (vec_ref[...].astype(jnp.float32) * mask_ref[...]).reshape(turns, held, n_beta)
    if padded != pairs:
        tail = pairs // PACK * PACK
        pairs_ref[:, tail:, :] = jnp.zeros((held, padded - tail, n_beta), jnp.bfloat16)

    def gathered(turn, k, index):
        value = None
        for c in range(chunks):
            row = jnp.broadcast_to(
                source_ref[turn, k : k + 1, c * LANES : (c + 1) * LANES], (index.shape[0], LANES)
            )
            found = jnp.take_along_axis(row, index % LANES if chunks > 1 else index, axis=1, mode="promise_in_bounds")
            value = found if value is None else jnp.where(index // LANES == c, found, value)
        return value

    def fill(turn, start, count):
        for c in range(chunks):
            index = addr_ref[pl.ds(start, count), c * LANES : (c + 1) * LANES]
            sign = sign_ref[pl.ds(start, count), c * LANES : (c + 1) * LANES].astype(jnp.float32)
            for k in range(held):
                pairs_ref[k, pl.ds(start, count), c * LANES : (c + 1) * LANES] = (
                    gathered(turn, k, index) * sign
                ).astype(jnp.bfloat16)

    factors = f_ref[...]

    def run(turn):
        def step(i, carry):
            fill(turn, pl.multiple_of(i * PACK, PACK), PACK)
            return carry

        lax.fori_loop(0, pairs // PACK, step, 0)
        if pairs % PACK:
            fill(turn, pairs // PACK * PACK, pairs % PACK)
        for k in range(held):
            t_ref[turn, k * aux : (k + 1) * aux, :] = jnp.dot(
                factors, pairs_ref[k, :pairs, :], preferred_element_type=jnp.float32
            )

    if turns == 1:
        run(0)
    else:
        pl.loop(0, turns)(run)

    partial = (
        jnp.dot(h_ref[...], t_ref[...].reshape(n_alpha * aux, n_beta), preferred_element_type=jnp.float32, precision=lax.Precision.HIGHEST)
        * mask_ref[...]
    )
    turn_ref[...] = partial.T
    devices = out_ref.shape[0]
    local = n_beta // devices
    out_ref[...] = jnp.concatenate(
        [turn_ref[pl.ds(k, devices, stride=local), :] for k in range(local)], axis=1
    )


def beta_side(vec, factors, h, mask, beta_addr, beta_sign, devices):
    aux, pairs = factors.shape
    n_alpha, n_beta = mask.shape
    padded = -(-pairs // PACK) * PACK
    held = max(k for k in range(1, n_alpha + 1) if n_alpha % k == 0 and k * padded * n_beta * 2 <= 12 * 2**20)
    return pl.pallas_call(
        beta_kernel,
        out_shape=jax.ShapeDtypeStruct((devices, n_beta // devices * n_alpha), jnp.float32),
        scratch_shapes=[
            pltpu.VMEM((n_alpha // held, held, n_beta), jnp.float32),
            pltpu.VMEM((held, padded, n_beta), jnp.bfloat16),
            pltpu.VMEM((n_alpha // held, held * aux, n_beta), jnp.float32),
            pltpu.VMEM((n_beta, n_alpha), jnp.float32),
        ],
        name="beta_side",
    )(vec, factors, h, mask, beta_addr.T, beta_sign.T)


def add_kernel(parts_ref, out_ref):
    total = jnp.sum(parts_ref[...], axis=0, keepdims=True)
    rows, columns = out_ref.shape
    for k in range(rows):
        out_ref[k : k + 1, :] = total[:, k * columns : (k + 1) * columns]


def on_device(
    vector,
    integrals,
    orbitals,
    alpha_addr,
    alpha_sign,
    beta_addr,
    beta_sign,
    seg_alpha,
    seg_beta,
    allowed,
):
    devices = lax.axis_size(AXES)
    n_beta = vector.shape[1]
    n_alpha = alpha_addr.shape[0]
    vec = lax.all_to_all(
        jnp.broadcast_to(vector, (devices,) + vector.shape), AXES, split_axis=0, concat_axis=0, tiled=True
    ).reshape(n_alpha, n_beta)
    factors = transform(integrals, orbitals)
    h, mask = alpha_side(factors, alpha_addr, alpha_sign, seg_alpha, seg_beta, allowed)
    partial = beta_side(vec, factors, h, mask, beta_addr, beta_sign, devices)
    parts = lax.all_to_all(partial, AXES, split_axis=0, concat_axis=0, tiled=True)
    return pl.pallas_call(
        add_kernel,
        out_shape=jax.ShapeDtypeStruct((n_beta // devices, n_alpha), jnp.float32),
        name="add_parts",
    )(parts)


def solution(mesh):
    rows = P(AXES, None)
    placed = (rows, P(AXES, None, None), P(), P(), P(), P(), P(), P(), P(), P())
    return jax.shard_map(on_device, mesh=mesh, in_specs=placed, out_specs=rows, check_vma=False)
```

```python
import functools

import jax
import jax.numpy as jnp
from jax import lax
from jax.experimental import pallas as pl
from jax.experimental.pallas import tpu as pltpu
from jax.sharding import PartitionSpec as P


AXES = ("grp", "blk")
LANES = 128
SUBLANES = 8
PACK = 16
UNROLL = 96
BLOCK = 50
AHEAD = 2
PREPARE_AT = 1
VMEM_LIMIT = 32 * 2**20
WIDE_LIMIT = 50 * 2**20
NT = (((1,), (1,)), ((), ()))
TN = (((0,), (0,)), ((), ()))


def placed_rows(values, before, total):
    width = values.shape[1]
    pieces = [jnp.zeros((before, width), values.dtype)] if before else []
    pieces.append(values)
    after = total - before - values.shape[0]
    if after:
        pieces.append(jnp.zeros((after, width), values.dtype))
    return jnp.concatenate(pieces, axis=0) if len(pieces) > 1 else values


def prepare(addr_ref, sign_ref, seg_a_ref, seg_b_ref, allowed_ref, hot_ref, mask_ref):
    side, rows, _ = hot_ref.shape
    halves, held, n_beta = mask_ref.shape
    n_alpha = addr_ref.shape[0]
    blocks = allowed_ref.shape[0]
    base = lax.axis_index("grp") % halves * held
    addr = addr_ref[...] - base
    sign = sign_ref[...].astype(jnp.float32)
    for q in range(side):
        for g in range(rows // n_alpha):
            hot_ref[q, g * n_alpha : (g + 1) * n_alpha, :] = jnp.where(addr == g * side + q, sign, 0.0).astype(
                jnp.bfloat16
            )
    hot_b = (lax.broadcasted_iota(jnp.int32, (blocks, n_beta), 0) == seg_b_ref[...]).astype(jnp.float32)
    hot_a = (lax.broadcasted_iota(jnp.int32, (blocks, n_alpha), 0) == seg_a_ref[...]).astype(jnp.float32)
    columns = jnp.dot(allowed_ref[...].astype(jnp.float32), hot_b, preferred_element_type=jnp.float32)
    mask_ref[...] = lax.dot_general(hot_a, columns, TN, preferred_element_type=jnp.float32).reshape(
        halves, held, n_beta
    )


def transform_kernel(
    big_ref,
    orb_any,
    addr_any,
    sign_any,
    seg_a_any,
    seg_b_any,
    allowed_any,
    out_ref,
    hot_ref,
    mask_ref,
    block_ref,
    orb_ref,
    addr_ref,
    sign_ref,
    seg_a_ref,
    seg_b_ref,
    allowed_ref,
    half_ref,
    turn_ref,
    big_sem,
    small_sem,
    *,
    sizes,
    half,
    stride,
):
    norb, nbas = orb_ref.shape
    groups = big_ref.shape[1] // PACK
    starts = [sum(sizes[:s]) for s in range(len(sizes))]

    def fetch(s):
        return [
            pltpu.make_async_copy(
                big_ref.at[pl.ds(part * half + starts[s], sizes[s])],
                block_ref.at[part, pl.ds(starts[s], sizes[s])],
                big_sem.at[s, part],
            )
            for part in range(2)
        ]

    small = [
        pltpu.make_async_copy(a, b, small_sem.at[k])
        for k, (a, b) in enumerate(
            (
                (orb_any, orb_ref),
                (addr_any, addr_ref),
                (sign_any, sign_ref),
                (seg_a_any, seg_a_ref),
                (seg_b_any, seg_b_ref),
                (allowed_any, allowed_ref),
            )
        )
    ]
    for copy in small:
        copy.start()
    for s in range(AHEAD):
        for copy in fetch(s):
            copy.start()
    small[0].wait()
    weights = orb_ref[...]
    for s, size in enumerate(sizes):
        for copy in fetch(s):
            copy.wait()
        if s + AHEAD < len(sizes):
            for copy in fetch(s + AHEAD):
                copy.start()
        cuts = [0, size // 2, size]
        total = [None, None]
        for part in range(2):
            for group in range(groups):
                placed = placed_rows(weights, (part * groups + group) * 32, LANES)
                for k in range(2):
                    block = block_ref[
                        part,
                        starts[s] + cuts[k] : starts[s] + cuts[k + 1],
                        group * PACK : (group + 1) * PACK,
                        :,
                    ].reshape(-1, nbas)
                    piece = lax.dot_general(block, placed, NT, preferred_element_type=jnp.float32)
                    total[k] = piece if total[k] is None else total[k] + piece
        for k in range(2):
            for row in range(cuts[k + 1] - cuts[k]):
                half_ref[pl.ds(starts[s] + cuts[k] + row, PACK, stride=stride), :] = total[k][
                    row * PACK : (row + 1) * PACK, :
                ]
        if s == PREPARE_AT:
            for copy in small[1:]:
                copy.wait()
            prepare(addr_ref, sign_ref, seg_a_ref, seg_b_ref, allowed_ref, hot_ref, mask_ref)
    both = jnp.concatenate(
        [placed_rows(weights[:, part * half : (part + 1) * half], 0, 32) for part in range(2)], axis=0
    )
    for r in range(PACK):
        right = half_ref[r * stride : r * stride + half, :].astype(jnp.bfloat16)
        sums = jnp.dot(both, right, preferred_element_type=jnp.float32)
        turn_ref[pl.ds(r, norb, stride=PACK), :] = sums[:norb] + pltpu.roll(sums[32 : 32 + norb], LANES - groups * 32, 1)
    flatten(turn_ref, out_ref, norb, groups)


def flatten(turn_ref, out_ref, norb, groups):
    lane = lax.broadcasted_iota(jnp.int32, (PACK, LANES), 1)
    pairs = norb * norb
    tiles = -(-(pairs + (groups - 1) * 32) // LANES)
    value = [[jnp.zeros((PACK, LANES), jnp.float32) for _ in range(tiles)] for _ in range(groups)]
    for i in range(norb):
        moved = pltpu.roll(turn_ref[i * PACK : (i + 1) * PACK, :], i * norb % LANES, 1)
        for group in range(groups):
            begin = i * norb + group * 32
            for tile in range(begin // LANES, (begin + norb - 1) // LANES + 1):
                low = begin - tile * LANES
                keep = (lane >= low) & (lane < low + norb)
                value[group][tile] = jnp.where(keep, moved, value[group][tile])
    for group in range(groups):
        shift = group * 32
        for tile in range(-(-pairs // LANES)):
            ends = min(LANES, pairs - tile * LANES)
            result = value[group][tile]
            if shift:
                result = pltpu.roll(result, LANES - shift, 1)
                if tile + 1 < tiles:
                    result = jnp.where(
                        lane < LANES - shift, result, pltpu.roll(value[group][tile + 1], LANES - shift, 1)
                    )
            out_ref[group * PACK : (group + 1) * PACK, tile * LANES : tile * LANES + ends] = result[:, :ends].astype(
                jnp.bfloat16
            )


def transform(integrals, orbitals, tables, hot_shape, mask_shape):
    aux, nbas, _ = integrals.shape
    norb = orbitals.shape[0]
    half = nbas // 2
    made = (jax.ShapeDtypeStruct(hot_shape, jnp.bfloat16), jax.ShapeDtypeStruct(mask_shape, jnp.float32))
    if aux % PACK or (aux // PACK) * 64 != LANES or norb > 32 or nbas % 2:
        half_done = jnp.einsum("jn,pmn->pjm", orbitals, integrals, preferred_element_type=jnp.float32).astype(
            jnp.bfloat16
        )
        factors = (
            jnp.einsum("im,pjm->pij", orbitals, half_done, preferred_element_type=jnp.float32)
            .reshape(aux, norb * norb)
            .astype(jnp.bfloat16)
        )
        return factors, *pl.pallas_call(prepare, out_shape=made, name="prepare")(*tables)
    sizes = block_sizes(half)
    stride = -(-half // 4) * 4
    stride += 4 if stride % SUBLANES == 0 else 0
    hbm = pl.BlockSpec(memory_space=pltpu.HBM)
    turned = jnp.transpose(integrals, (1, 0, 2))
    orbitals, *tables = (pltpu.with_memory_space_constraint(t, pltpu.HBM) for t in (orbitals, *tables))
    return pl.pallas_call(
        functools.partial(transform_kernel, sizes=sizes, half=half, stride=stride),
        in_specs=[hbm] * (2 + len(tables)),
        out_shape=(jax.ShapeDtypeStruct((aux, norb * norb), jnp.bfloat16),) + made,
        scratch_shapes=[
            pltpu.VMEM((2, half, aux, nbas), jnp.bfloat16),
            pltpu.VMEM(orbitals.shape, orbitals.dtype),
        ]
        + [pltpu.VMEM(t.shape, t.dtype) for t in tables]
        + [
            pltpu.VMEM((PACK * stride, LANES), jnp.float32),
            pltpu.VMEM((norb * PACK, LANES), jnp.float32),
            pltpu.SemaphoreType.DMA((len(sizes), 2)),
            pltpu.SemaphoreType.DMA((1 + len(tables),)),
        ],
        cost_estimate=pl.CostEstimate(
            flops=4 * aux * nbas * nbas * LANES, transcendentals=0, bytes_accessed=2 * aux * nbas * nbas
        ),
        compiler_params=pltpu.CompilerParams(vmem_limit_bytes=WIDE_LIMIT),
        name="transform",
    )(turned, orbitals, *tables)


def block_sizes(half):
    sizes, left = [], half
    while left:
        size = min(left, BLOCK if left > BLOCK else 25)
        sizes.append(size)
        left -= size
    return tuple(sizes)


def split(value):
    high = value.astype(jnp.bfloat16)
    return high, (value - high.astype(jnp.float32)).astype(jnp.bfloat16)


def set_sources(vec_ref, mask_ref, source_ref):
    halves, mine, _ = mask_ref.shape
    held = source_ref.shape[1]
    core = lax.axis_index("grp") % halves
    for k in range(mine):
        source_ref[k // held, k % held : k % held + 1, :] = (
            vec_ref[core * mine + k].astype(jnp.float32) * mask_ref[core, k : k + 1, :]
        )


def gather_pairs(turn, addr_ref, sign_ref, source_ref, pairs_ref):
    pairs, n_beta = addr_ref.shape
    held = source_ref.shape[1]
    chunks = n_beta // LANES

    def gathered(k, index):
        value = None
        for c in range(chunks):
            row = jnp.broadcast_to(
                source_ref[turn, k : k + 1, c * LANES : (c + 1) * LANES], (index.shape[0], LANES)
            )
            found = jnp.take_along_axis(row, index % LANES if chunks > 1 else index, axis=1, mode="promise_in_bounds")
            value = found if value is None else jnp.where(index // LANES == c, found, value)
        return value

    def fill(start, count):
        for c in range(chunks):
            index = addr_ref[pl.ds(start, count), c * LANES : (c + 1) * LANES]
            sign = sign_ref[pl.ds(start, count), c * LANES : (c + 1) * LANES].astype(jnp.float32)
            for k in range(held):
                place = k * n_beta + c * LANES
                pairs_ref[pl.ds(start, count), place : place + LANES] = (gathered(k, index) * sign).astype(jnp.bfloat16)

    together = pairs // SUBLANES
    unroll = max(
        u for u in range(1, together + 1) if together % u == 0 and (u == 1 or u * held * chunks**2 <= UNROLL)
    )

    def step(i, carry):
        for u in range(unroll):
            fill(pl.multiple_of((i * unroll + u) * SUBLANES, SUBLANES), SUBLANES)
        return carry

    lax.fori_loop(0, together // unroll, step, 0)
    if pairs % SUBLANES:
        fill(together * SUBLANES, pairs % SUBLANES)


def set_alpha(factors, hot_ref, h_ref):
    side = hot_ref.shape[0]
    n_alpha, width = h_ref.shape
    total = None
    for q in range(side):
        part = lax.dot_general(
            hot_ref[q],
            placed_rows(factors, q * factors.shape[0], LANES),
            NT,
            preferred_element_type=jnp.float32,
        )
        total = part if total is None else total + part
    for g in range(width // LANES):
        h_ref[:, g * LANES : (g + 1) * LANES] = total[g * n_alpha : (g + 1) * n_alpha, :]


def contract_pairs(turn, factors, pairs_ref, t_ref, n_beta):
    aux, pairs = factors.shape
    held = t_ref.shape[1] // aux
    wide = max(1, 512 // n_beta)
    for first in range(0, held, wide):
        last = min(first + wide, held)
        part = jnp.dot(factors, pairs_ref[:pairs, first * n_beta : last * n_beta], preferred_element_type=jnp.float32)
        for k in range(first, last):
            t_ref[turn, k * aux : (k + 1) * aux, :] = part[:, (k - first) * n_beta : (k - first + 1) * n_beta]


def finish(h_ref, t_ref, mask_ref, turn_ref, out_ref):
    n_alpha, width = h_ref.shape
    n_beta = mask_ref.shape[2]
    h_high, h_low = split(h_ref[...])
    t_high, t_low = split(t_ref[...].reshape(width, n_beta))
    both = jnp.dot(jnp.concatenate([h_high, h_low], axis=0), t_high, preferred_element_type=jnp.float32)
    rest = jnp.dot(h_high, t_low, preferred_element_type=jnp.float32)
    partial = both[:n_alpha] + (both[n_alpha:] + rest)
    turn_ref[...] = (partial * mask_ref[...].reshape(n_alpha, n_beta)).T
    devices = out_ref.shape[0]
    local = n_beta // devices
    out_ref[...] = jnp.concatenate(
        [turn_ref[pl.ds(k, devices, stride=local), :] for k in range(local)], axis=1
    )


def gather_kernel(vec_ref, mask_ref, addr_ref, sign_ref, pairs_ref, source_ref):
    set_sources(vec_ref, mask_ref, source_ref)
    gather_pairs(0, addr_ref, sign_ref, source_ref, pairs_ref)


def contract_kernel(own_ref, other_ref, hot_ref, mask_ref, pairs_ref, out_ref, h_ref, t_ref, turn_ref):
    factors = jnp.concatenate([own_ref[...], other_ref[...]], axis=0)
    set_alpha(factors, hot_ref, h_ref)
    contract_pairs(0, factors, pairs_ref, t_ref, mask_ref.shape[2])
    finish(h_ref, t_ref, mask_ref, turn_ref, out_ref)


def beta_kernel(
    vec_ref,
    own_ref,
    other_ref,
    hot_ref,
    mask_ref,
    addr_ref,
    sign_ref,
    out_ref,
    source_ref,
    pairs_ref,
    h_ref,
    t_ref,
    turn_ref,
):
    set_sources(vec_ref, mask_ref, source_ref)
    factors = jnp.concatenate([own_ref[...], other_ref[...]], axis=0)
    set_alpha(factors, hot_ref, h_ref)

    @pl.loop(0, source_ref.shape[0])
    def _(turn):
        gather_pairs(turn, addr_ref, sign_ref, source_ref, pairs_ref)
        contract_pairs(turn, factors, pairs_ref, t_ref, mask_ref.shape[2])

    finish(h_ref, t_ref, mask_ref, turn_ref, out_ref)


def beta_side(vec, own, hot, mask, beta_addr, beta_sign, devices):
    aux, pairs = own.shape
    halves, mine, n_beta = mask.shape
    groups = lax.axis_size("grp")
    other = lax.ppermute(own, "grp", [(g, g ^ 1) for g in range(groups)])
    addr, sign = beta_addr.T, beta_sign.T
    held = max(k for k in range(1, mine + 1) if mine % k == 0 and k * pairs * n_beta * 2 <= 12 * 2**20)
    params = pltpu.CompilerParams(vmem_limit_bytes=VMEM_LIMIT)
    made = jax.ShapeDtypeStruct((devices, n_beta // devices * halves * mine), jnp.float32)
    source = pltpu.VMEM((mine // held, held, n_beta), jnp.float32)
    product = jax.ShapeDtypeStruct((pairs, held * n_beta), jnp.bfloat16)
    sums = [
        pltpu.VMEM((halves * mine, mine * 2 * aux), jnp.float32),
        pltpu.VMEM((mine // held, held * 2 * aux, n_beta), jnp.float32),
        pltpu.VMEM((n_beta, halves * mine), jnp.float32),
    ]
    if held == mine:
        terms = pl.pallas_call(
            gather_kernel,
            out_shape=product,
            scratch_shapes=[source],
            compiler_params=params,
            cost_estimate=pl.CostEstimate(flops=0, transcendentals=0, bytes_accessed=8 * pairs * mine * n_beta),
            name="gather",
        )(vec, mask, addr, sign)
        return pl.pallas_call(
            contract_kernel, out_shape=made, scratch_shapes=sums, compiler_params=params, name="contract"
        )(own, other, hot, mask, terms)
    return pl.pallas_call(
        beta_kernel,
        out_shape=made,
        scratch_shapes=[source, pltpu.VMEM(product.shape, product.dtype)] + sums,
        compiler_params=params,
        name="beta_side",
    )(vec, own, other, hot, mask, addr, sign)


def add_kernel(parts_ref, out_ref):
    total = jnp.sum(parts_ref[...], axis=0, keepdims=True)
    rows, columns = out_ref.shape
    for k in range(rows):
        out_ref[k : k + 1, :] = total[:, k * columns : (k + 1) * columns]


def on_device(
    vector,
    integrals,
    orbitals,
    alpha_addr,
    alpha_sign,
    beta_addr,
    beta_sign,
    seg_alpha,
    seg_beta,
    allowed,
):
    devices = lax.axis_size(AXES)
    n_beta = vector.shape[1]
    n_alpha, pairs = alpha_addr.shape
    mine = n_alpha // 2
    side = LANES // (2 * integrals.shape[0])
    vec = lax.all_to_all(
        jnp.broadcast_to(vector, (devices,) + vector.shape), AXES, split_axis=0, concat_axis=0, tiled=True
    ).reshape(n_alpha, 1, n_beta)
    tables = (alpha_addr, alpha_sign, seg_alpha.reshape(1, -1), seg_beta.reshape(1, -1), allowed)
    own, hot, mask = transform(integrals, orbitals, tables, (side, mine // side * n_alpha, pairs), (2, mine, n_beta))
    partial = beta_side(vec, own, hot, mask, beta_addr, beta_sign, devices)
    parts = lax.all_to_all(partial, AXES, split_axis=0, concat_axis=0, tiled=True)
    return pl.pallas_call(
        add_kernel,
        out_shape=jax.ShapeDtypeStruct((n_beta // devices, n_alpha), jnp.float32),
        compiler_params=pltpu.CompilerParams(vmem_limit_bytes=VMEM_LIMIT),
        name="add_parts",
    )(parts)


def solution(mesh):
    rows = P(AXES, None)
    placed = (rows, P(AXES, None, None), P(), P(), P(), P(), P(), P(), P(), P())
    return jax.shard_map(on_device, mesh=mesh, in_specs=placed, out_specs=rows, check_vma=False)
```

```python
import functools

import jax
import jax.numpy as jnp
from jax import lax
from jax.experimental import pallas as pl
from jax.experimental.pallas import tpu as pltpu
from jax.sharding import PartitionSpec as P


AXES = ("grp", "blk")
LANES = 128
SUBLANES = 8
PACK = 16
UNROLL = 672
AHEAD = 3
HEAD = 25
BLOCK = 50
PREPARE_AT = 1
VMEM_LIMIT = 32 * 2**20
WIDE_LIMIT = 50 * 2**20
NT = (((1,), (1,)), ((), ()))
TN = (((0,), (0,)), ((), ()))


def placed_rows(values, before, total):
    width = values.shape[1]
    pieces = [jnp.zeros((before, width), values.dtype)] if before else []
    pieces.append(values)
    after = total - before - values.shape[0]
    if after:
        pieces.append(jnp.zeros((after, width), values.dtype))
    return jnp.concatenate(pieces, axis=0) if len(pieces) > 1 else values


def prepare(addr_ref, sign_ref, seg_a_ref, seg_b_ref, allowed_ref, hot_ref, mask_ref):
    side, rows, _ = hot_ref.shape
    halves, held, n_beta = mask_ref.shape
    n_alpha = addr_ref.shape[0]
    blocks = allowed_ref.shape[0]
    base = lax.axis_index("grp") % halves * held
    addr = addr_ref[...] - base
    sign = sign_ref[...].astype(jnp.float32)
    for q in range(side):
        for g in range(rows // n_alpha):
            hot_ref[q, g * n_alpha : (g + 1) * n_alpha, :] = jnp.where(addr == g * side + q, sign, 0.0).astype(
                jnp.bfloat16
            )
    hot_b = (lax.broadcasted_iota(jnp.int32, (blocks, n_beta), 0) == seg_b_ref[...]).astype(jnp.float32)
    hot_a = (lax.broadcasted_iota(jnp.int32, (blocks, n_alpha), 0) == seg_a_ref[...]).astype(jnp.float32)
    columns = jnp.dot(allowed_ref[...].astype(jnp.float32), hot_b, preferred_element_type=jnp.float32)
    mask_ref[...] = lax.dot_general(hot_a, columns, TN, preferred_element_type=jnp.float32).reshape(
        halves, held, n_beta
    )


def start_kernel(vector_any, big_ref, out_any, head_ref, vector_ref, copy_ref, sem):
    size = head_ref.shape[1]
    vector = pltpu.make_async_copy(vector_any, vector_ref, sem.at[0])
    head = [
        pltpu.make_async_copy(
            big_ref.at[pl.ds(part * (big_ref.shape[0] // 2), size)], head_ref.at[part], sem.at[1 + part]
        )
        for part in range(2)
    ]
    out = pltpu.make_async_copy(copy_ref, out_any, sem.at[3])
    vector.start()
    for copy in head:
        copy.start()
    vector.wait()
    copy_ref[...] = jnp.broadcast_to(vector_ref[...][None], copy_ref.shape)
    out.start()
    out.wait()
    for copy in head:
        copy.wait()


def start(vector, integrals, devices):
    aux, nbas, _ = integrals.shape
    if not fits(integrals):
        return jnp.broadcast_to(vector, (devices,) + vector.shape), None
    hbm = pl.BlockSpec(memory_space=pltpu.HBM)
    vector, turned = (
        pltpu.with_memory_space_constraint(t, pltpu.HBM) for t in (vector, jnp.transpose(integrals, (1, 0, 2)))
    )
    return pl.pallas_call(
        start_kernel,
        in_specs=[hbm] * 2,
        out_specs=(hbm, pl.BlockSpec(memory_space=pltpu.VMEM)),
        out_shape=(
            jax.ShapeDtypeStruct((devices,) + vector.shape, vector.dtype),
            jax.ShapeDtypeStruct((2, min(HEAD, nbas // 2), aux, nbas), integrals.dtype),
        ),
        scratch_shapes=[
            pltpu.VMEM(vector.shape, vector.dtype),
            pltpu.VMEM((devices,) + vector.shape, vector.dtype),
            pltpu.SemaphoreType.DMA((4,)),
        ],
        compiler_params=pltpu.CompilerParams(vmem_limit_bytes=VMEM_LIMIT),
        name="start",
    )(vector, turned)


def fits(integrals):
    aux, nbas, _ = integrals.shape
    return aux % PACK == 0 and aux // PACK * 64 == LANES and nbas % 2 == 0


def transform_kernel(
    big_ref,
    head_ref,
    orb_any,
    addr_any,
    sign_any,
    seg_a_any,
    seg_b_any,
    allowed_any,
    out_ref,
    hot_ref,
    mask_ref,
    block_ref,
    orb_ref,
    addr_ref,
    sign_ref,
    seg_a_ref,
    seg_b_ref,
    allowed_ref,
    half_ref,
    turn_ref,
    big_sem,
    small_sem,
    *,
    sizes,
    half,
    stride,
):
    norb, nbas = orb_ref.shape
    groups = big_ref.shape[1] // PACK
    starts = [sum(sizes[:s]) for s in range(len(sizes))]
    first = head_ref.shape[1]

    def fetch(s):
        return [
            pltpu.make_async_copy(
                big_ref.at[pl.ds(part * half + starts[s], sizes[s])],
                block_ref.at[part, pl.ds(starts[s] - first, sizes[s])],
                big_sem.at[s, part],
            )
            for part in range(2)
        ]

    small = [
        pltpu.make_async_copy(a, b, small_sem.at[k])
        for k, (a, b) in enumerate(
            (
                (orb_any, orb_ref),
                (addr_any, addr_ref),
                (sign_any, sign_ref),
                (seg_a_any, seg_a_ref),
                (seg_b_any, seg_b_ref),
                (allowed_any, allowed_ref),
            )
        )
    ]
    for copy in small:
        copy.start()
    for s in range(1, 1 + AHEAD):
        for copy in fetch(s):
            copy.start()
    small[0].wait()
    weights = orb_ref[...]
    for s, size in enumerate(sizes):
        source, begin = (block_ref, starts[s] - first) if s else (head_ref, 0)
        for copy in fetch(s) if s else ():
            copy.wait()
        if 0 < s < len(sizes) - AHEAD:
            for copy in fetch(s + AHEAD):
                copy.start()
        cuts = [0, size // 2, size]
        total = [None, None]
        for part in range(2):
            for group in range(groups):
                placed = placed_rows(weights, (part * groups + group) * 32, LANES)
                for k in range(2):
                    block = source[
                        part,
                        begin + cuts[k] : begin + cuts[k + 1],
                        group * PACK : (group + 1) * PACK,
                        :,
                    ].reshape(-1, nbas)
                    piece = lax.dot_general(block, placed, NT, preferred_element_type=jnp.float32)
                    total[k] = piece if total[k] is None else total[k] + piece
        for k in range(2):
            for row in range(cuts[k + 1] - cuts[k]):
                half_ref[pl.ds(starts[s] + cuts[k] + row, PACK, stride=stride), :] = total[k][
                    row * PACK : (row + 1) * PACK, :
                ]
        if s == PREPARE_AT:
            for copy in small[1:]:
                copy.wait()
            prepare(addr_ref, sign_ref, seg_a_ref, seg_b_ref, allowed_ref, hot_ref, mask_ref)
    both = jnp.concatenate(
        [placed_rows(weights[:, part * half : (part + 1) * half], 0, 32) for part in range(2)], axis=0
    )
    for r in range(PACK):
        right = half_ref[r * stride : r * stride + half, :].astype(jnp.bfloat16)
        sums = jnp.dot(both, right, preferred_element_type=jnp.float32)
        turn_ref[pl.ds(r, norb, stride=PACK), :] = sums[:norb] + pltpu.roll(sums[32 : 32 + norb], LANES - groups * 32, 1)
    flatten(turn_ref, out_ref, norb, groups)


def flatten(turn_ref, out_ref, norb, groups):
    lane = lax.broadcasted_iota(jnp.int32, (PACK, LANES), 1)
    pairs = norb * norb
    tiles = -(-(pairs + (groups - 1) * 32) // LANES)
    value = [[jnp.zeros((PACK, LANES), jnp.float32) for _ in range(tiles)] for _ in range(groups)]
    for i in range(norb):
        moved = pltpu.roll(turn_ref[i * PACK : (i + 1) * PACK, :], i * norb % LANES, 1)
        for group in range(groups):
            begin = i * norb + group * 32
            for tile in range(begin // LANES, (begin + norb - 1) // LANES + 1):
                low = begin - tile * LANES
                keep = (lane >= low) & (lane < low + norb)
                value[group][tile] = jnp.where(keep, moved, value[group][tile])
    for group in range(groups):
        shift = group * 32
        for tile in range(-(-pairs // LANES)):
            ends = min(LANES, pairs - tile * LANES)
            result = value[group][tile]
            if shift:
                result = pltpu.roll(result, LANES - shift, 1)
                if tile + 1 < tiles:
                    result = jnp.where(
                        lane < LANES - shift, result, pltpu.roll(value[group][tile + 1], LANES - shift, 1)
                    )
            out_ref[group * PACK : (group + 1) * PACK, tile * LANES : tile * LANES + ends] = result[:, :ends].astype(
                jnp.bfloat16
            )


def transform(integrals, head, orbitals, tables, hot_shape, mask_shape):
    aux, nbas, _ = integrals.shape
    norb = orbitals.shape[0]
    half = nbas // 2
    made = (jax.ShapeDtypeStruct(hot_shape, jnp.bfloat16), jax.ShapeDtypeStruct(mask_shape, jnp.float32))
    if head is None:
        half_done = jnp.einsum("jn,pmn->pjm", orbitals, integrals, preferred_element_type=jnp.float32).astype(
            jnp.bfloat16
        )
        factors = (
            jnp.einsum("im,pjm->pij", orbitals, half_done, preferred_element_type=jnp.float32)
            .reshape(aux, norb * norb)
            .astype(jnp.bfloat16)
        )
        return factors, *pl.pallas_call(prepare, out_shape=made, name="prepare")(*tables)
    sizes = (head.shape[1],) + block_sizes(half - head.shape[1])
    stride = -(-half // 4) * 4
    stride += 4 if stride % SUBLANES == 0 else 0
    hbm = pl.BlockSpec(memory_space=pltpu.HBM)
    turned = jnp.transpose(integrals, (1, 0, 2))
    turned, orbitals, *tables = (
        pltpu.with_memory_space_constraint(t, pltpu.HBM) for t in (turned, orbitals, *tables)
    )
    return pl.pallas_call(
        functools.partial(transform_kernel, sizes=sizes, half=half, stride=stride),
        in_specs=[hbm, pl.BlockSpec(memory_space=pltpu.VMEM)] + [hbm] * (1 + len(tables)),
        out_shape=(jax.ShapeDtypeStruct((aux, norb * norb), jnp.bfloat16),) + made,
        scratch_shapes=[
            pltpu.VMEM((2, half - sizes[0], aux, nbas), jnp.bfloat16),
            pltpu.VMEM(orbitals.shape, orbitals.dtype),
        ]
        + [pltpu.VMEM(t.shape, t.dtype) for t in tables]
        + [
            pltpu.VMEM((PACK * stride, LANES), jnp.float32),
            pltpu.VMEM((norb * PACK, LANES), jnp.float32),
            pltpu.SemaphoreType.DMA((len(sizes), 2)),
            pltpu.SemaphoreType.DMA((1 + len(tables),)),
        ],
        cost_estimate=pl.CostEstimate(
            flops=4 * aux * nbas * nbas * LANES, transcendentals=0, bytes_accessed=2 * aux * nbas * nbas
        ),
        compiler_params=pltpu.CompilerParams(vmem_limit_bytes=WIDE_LIMIT),
        name="transform",
    )(turned, head, orbitals, *tables)


def block_sizes(rows):
    sizes, left = [], rows
    while left:
        size = min(left, BLOCK if left > BLOCK else BLOCK // 2)
        sizes.append(size)
        left -= size
    return tuple(sizes)


def split(value):
    high = value.astype(jnp.bfloat16)
    return high, (value - high.astype(jnp.float32)).astype(jnp.bfloat16)


def set_sources(vec_ref, mask_ref, source_ref):
    halves, mine, _ = mask_ref.shape
    held = source_ref.shape[1]
    core = lax.axis_index("grp") % halves
    for k in range(mine):
        source_ref[k // held, k % held : k % held + 1, :] = (
            vec_ref[core * mine + k].astype(jnp.float32) * mask_ref[core, k : k + 1, :]
        )


def gather_pairs(turn, addr_ref, sign_ref, source_ref, pairs_ref):
    pairs, n_beta = addr_ref.shape
    held = source_ref.shape[1]
    chunks = n_beta // LANES

    def gathered(k, index):
        value = None
        for c in range(chunks):
            row = jnp.broadcast_to(
                source_ref[turn, k : k + 1, c * LANES : (c + 1) * LANES], (index.shape[0], LANES)
            )
            found = jnp.take_along_axis(row, index % LANES if chunks > 1 else index, axis=1, mode="promise_in_bounds")
            value = found if value is None else jnp.where(index // LANES == c, found, value)
        return value

    def fill(start, count):
        for c in range(chunks):
            index = addr_ref[pl.ds(start, count), c * LANES : (c + 1) * LANES]
            sign = sign_ref[pl.ds(start, count), c * LANES : (c + 1) * LANES].astype(jnp.float32)
            for k in range(held):
                place = k * n_beta + c * LANES
                pairs_ref[pl.ds(start, count), place : place + LANES] = (gathered(k, index) * sign).astype(jnp.bfloat16)

    together = pairs // SUBLANES
    unroll = max(
        u for u in range(1, together + 1) if together % u == 0 and (u == 1 or u * held * chunks**2 <= UNROLL)
    )

    def step(i, carry):
        for u in range(unroll):
            fill(pl.multiple_of((i * unroll + u) * SUBLANES, SUBLANES), SUBLANES)
        return carry

    lax.fori_loop(0, together // unroll, step, 0)
    if pairs % SUBLANES:
        fill(together * SUBLANES, pairs % SUBLANES)


def set_alpha(factors, hot_ref, h_ref):
    side = hot_ref.shape[0]
    n_alpha, width = h_ref.shape
    total = None
    for q in range(side):
        part = lax.dot_general(
            hot_ref[q],
            placed_rows(factors, q * factors.shape[0], LANES),
            NT,
            preferred_element_type=jnp.float32,
        )
        total = part if total is None else total + part
    for g in range(width // LANES):
        h_ref[:, g * LANES : (g + 1) * LANES] = total[g * n_alpha : (g + 1) * n_alpha, :]


def contract_pairs(turn, factors, pairs_ref, t_ref, n_beta):
    aux, pairs = factors.shape
    held = t_ref.shape[1] // aux
    wide = max(1, 256 // n_beta)
    for first in range(0, held, wide):
        last = min(first + wide, held)
        part = jnp.dot(factors, pairs_ref[:pairs, first * n_beta : last * n_beta], preferred_element_type=jnp.float32)
        for k in range(first, last):
            t_ref[turn, k * aux : (k + 1) * aux, :] = part[:, (k - first) * n_beta : (k - first + 1) * n_beta]


def finish(h_ref, t_ref, mask_ref, turn_ref, out_ref):
    n_alpha, width = h_ref.shape
    n_beta = mask_ref.shape[2]
    h_high, h_low = split(h_ref[...])
    t_high, t_low = split(t_ref[...].reshape(width, n_beta))
    both = jnp.dot(jnp.concatenate([h_high, h_low], axis=0), t_high, preferred_element_type=jnp.float32)
    rest = jnp.dot(h_high, t_low, preferred_element_type=jnp.float32)
    partial = both[:n_alpha] + (both[n_alpha:] + rest)
    turn_ref[...] = (partial * mask_ref[...].reshape(n_alpha, n_beta)).T
    devices = out_ref.shape[0]
    local = n_beta // devices
    out_ref[...] = jnp.concatenate(
        [turn_ref[pl.ds(k, devices, stride=local), :] for k in range(local)], axis=1
    )


def gather_kernel(vec_ref, mask_ref, addr_ref, sign_ref, pairs_ref, source_ref):
    set_sources(vec_ref, mask_ref, source_ref)
    gather_pairs(0, addr_ref, sign_ref, source_ref, pairs_ref)


def contract_kernel(own_ref, other_ref, hot_ref, mask_ref, pairs_ref, out_ref, h_ref, t_ref, turn_ref):
    factors = jnp.concatenate([own_ref[...], other_ref[...]], axis=0)
    set_alpha(factors, hot_ref, h_ref)
    contract_pairs(0, factors, pairs_ref, t_ref, mask_ref.shape[2])
    finish(h_ref, t_ref, mask_ref, turn_ref, out_ref)


def beta_kernel(
    vec_ref,
    own_ref,
    other_ref,
    hot_ref,
    mask_ref,
    addr_ref,
    sign_ref,
    out_ref,
    source_ref,
    pairs_ref,
    h_ref,
    t_ref,
    turn_ref,
):
    set_sources(vec_ref, mask_ref, source_ref)
    factors = jnp.concatenate([own_ref[...], other_ref[...]], axis=0)
    set_alpha(factors, hot_ref, h_ref)

    @pl.loop(0, source_ref.shape[0])
    def _(turn):
        gather_pairs(turn, addr_ref, sign_ref, source_ref, pairs_ref)
        contract_pairs(turn, factors, pairs_ref, t_ref, mask_ref.shape[2])

    finish(h_ref, t_ref, mask_ref, turn_ref, out_ref)


def beta_side(vec, own, hot, mask, beta_addr, beta_sign, devices):
    aux, pairs = own.shape
    halves, mine, n_beta = mask.shape
    groups = lax.axis_size("grp")
    other = lax.ppermute(own, "grp", [(g, g ^ 1) for g in range(groups)])
    addr, sign = beta_addr.T, beta_sign.T
    held = max(k for k in range(1, mine + 1) if mine % k == 0 and k * pairs * n_beta * 2 <= 12 * 2**20)
    params = pltpu.CompilerParams(vmem_limit_bytes=VMEM_LIMIT)
    made = jax.ShapeDtypeStruct((devices, n_beta // devices * halves * mine), jnp.float32)
    source = pltpu.VMEM((mine // held, held, n_beta), jnp.float32)
    product = jax.ShapeDtypeStruct((pairs, held * n_beta), jnp.bfloat16)
    sums = [
        pltpu.VMEM((halves * mine, mine * 2 * aux), jnp.float32),
        pltpu.VMEM((mine // held, held * 2 * aux, n_beta), jnp.float32),
        pltpu.VMEM((n_beta, halves * mine), jnp.float32),
    ]
    if held == mine:
        terms = pl.pallas_call(
            gather_kernel,
            out_shape=product,
            scratch_shapes=[source],
            compiler_params=params,
            cost_estimate=pl.CostEstimate(flops=0, transcendentals=0, bytes_accessed=8 * pairs * mine * n_beta),
            name="gather",
        )(vec, mask, addr, sign)
        return pl.pallas_call(
            contract_kernel, out_shape=made, scratch_shapes=sums, compiler_params=params, name="contract"
        )(own, other, hot, mask, terms)
    return pl.pallas_call(
        beta_kernel,
        out_shape=made,
        scratch_shapes=[source, pltpu.VMEM(product.shape, product.dtype)] + sums,
        compiler_params=params,
        name="beta_side",
    )(vec, own, other, hot, mask, addr, sign)


def add_kernel(parts_ref, out_ref):
    total = jnp.sum(parts_ref[...], axis=0, keepdims=True)
    rows, columns = out_ref.shape
    for k in range(rows):
        out_ref[k : k + 1, :] = total[:, k * columns : (k + 1) * columns]


def on_device(
    vector,
    integrals,
    orbitals,
    alpha_addr,
    alpha_sign,
    beta_addr,
    beta_sign,
    seg_alpha,
    seg_beta,
    allowed,
):
    devices = lax.axis_size(AXES)
    n_beta = vector.shape[1]
    n_alpha, pairs = alpha_addr.shape
    mine = n_alpha // 2
    side = LANES // (2 * integrals.shape[0])
    rows, head = start(vector, integrals, devices)
    vec = lax.all_to_all(
        rows, AXES, split_axis=0, concat_axis=0, tiled=True
    ).reshape(n_alpha, 1, n_beta)
    tables = (alpha_addr, alpha_sign, seg_alpha.reshape(1, -1), seg_beta.reshape(1, -1), allowed)
    own, hot, mask = transform(
        integrals, head, orbitals, tables, (side, mine // side * n_alpha, pairs), (2, mine, n_beta)
    )
    partial = beta_side(vec, own, hot, mask, beta_addr, beta_sign, devices)
    parts = lax.all_to_all(partial, AXES, split_axis=0, concat_axis=0, tiled=True)
    return pl.pallas_call(
        add_kernel,
        out_shape=jax.ShapeDtypeStruct((n_beta // devices, n_alpha), jnp.float32),
        compiler_params=pltpu.CompilerParams(vmem_limit_bytes=VMEM_LIMIT),
        name="add_parts",
    )(parts)


def solution(mesh):
    rows = P(AXES, None)
    placed = (rows, P(AXES, None, None), P(), P(), P(), P(), P(), P(), P(), P())
    return jax.shard_map(on_device, mesh=mesh, in_specs=placed, out_specs=rows, check_vma=False)
```

```python
import functools

import jax
import jax.numpy as jnp
from jax import lax
from jax.experimental import pallas as pl
from jax.experimental.pallas import tpu as pltpu
from jax.sharding import PartitionSpec as P


AXES = ("grp", "blk")
LANES = 128
SUBLANES = 8
PACK = 16
UNROLL = 1344
AHEAD = 3
HEAD = 25
BLOCK = 50
PREPARE_AT = 1
VMEM_LIMIT = 32 * 2**20
WIDE_LIMIT = 50 * 2**20
NT = (((1,), (1,)), ((), ()))
TN = (((0,), (0,)), ((), ()))


def placed_rows(values, before, total):
    width = values.shape[1]
    pieces = [jnp.zeros((before, width), values.dtype)] if before else []
    pieces.append(values)
    after = total - before - values.shape[0]
    if after:
        pieces.append(jnp.zeros((after, width), values.dtype))
    return jnp.concatenate(pieces, axis=0) if len(pieces) > 1 else values


def prepare(addr_ref, sign_ref, seg_a_ref, seg_b_ref, allowed_ref, hot_ref, mask_ref):
    side, rows, _ = hot_ref.shape
    halves, held, n_beta = mask_ref.shape
    n_alpha = addr_ref.shape[0]
    blocks = allowed_ref.shape[0]
    base = lax.axis_index("grp") % halves * held
    addr = addr_ref[...] - base
    sign = sign_ref[...].astype(jnp.float32)
    for q in range(side):
        for g in range(rows // n_alpha):
            hot_ref[q, g * n_alpha : (g + 1) * n_alpha, :] = jnp.where(addr == g * side + q, sign, 0.0).astype(
                jnp.bfloat16
            )
    hot_b = (lax.broadcasted_iota(jnp.int32, (blocks, n_beta), 0) == seg_b_ref[...]).astype(jnp.float32)
    hot_a = (lax.broadcasted_iota(jnp.int32, (blocks, n_alpha), 0) == seg_a_ref[...]).astype(jnp.float32)
    columns = jnp.dot(allowed_ref[...].astype(jnp.float32), hot_b, preferred_element_type=jnp.float32)
    mask_ref[...] = lax.dot_general(hot_a, columns, TN, preferred_element_type=jnp.float32).reshape(
        halves, held, n_beta
    )


def start_kernel(vector_any, big_ref, out_any, head_ref, vector_ref, copy_ref, sem):
    size = head_ref.shape[1]
    vector = pltpu.make_async_copy(vector_any, vector_ref, sem.at[0])
    head = [
        pltpu.make_async_copy(
            big_ref.at[pl.ds(part * (big_ref.shape[0] // 2), size)], head_ref.at[part], sem.at[1 + part]
        )
        for part in range(2)
    ]
    out = pltpu.make_async_copy(copy_ref, out_any, sem.at[3])
    vector.start()
    for copy in head:
        copy.start()
    vector.wait()
    copy_ref[...] = jnp.broadcast_to(vector_ref[...][None], copy_ref.shape)
    out.start()
    out.wait()
    for copy in head:
        copy.wait()


def start(vector, integrals, devices):
    aux, nbas, _ = integrals.shape
    if not fits(integrals):
        return jnp.broadcast_to(vector, (devices,) + vector.shape), None
    hbm = pl.BlockSpec(memory_space=pltpu.HBM)
    vector, turned = (
        pltpu.with_memory_space_constraint(t, pltpu.HBM) for t in (vector, jnp.transpose(integrals, (1, 0, 2)))
    )
    return pl.pallas_call(
        start_kernel,
        in_specs=[hbm] * 2,
        out_specs=(hbm, pl.BlockSpec(memory_space=pltpu.VMEM)),
        out_shape=(
            jax.ShapeDtypeStruct((devices,) + vector.shape, vector.dtype),
            jax.ShapeDtypeStruct((2, min(HEAD, nbas // 2), aux, nbas), integrals.dtype),
        ),
        scratch_shapes=[
            pltpu.VMEM(vector.shape, vector.dtype),
            pltpu.VMEM((devices,) + vector.shape, vector.dtype),
            pltpu.SemaphoreType.DMA((4,)),
        ],
        compiler_params=pltpu.CompilerParams(vmem_limit_bytes=VMEM_LIMIT),
        name="start",
    )(vector, turned)


def fits(integrals):
    aux, nbas, _ = integrals.shape
    return aux % PACK == 0 and aux // PACK * 64 == LANES and nbas % 2 == 0


def transform_kernel(
    big_ref,
    head_ref,
    b_addr_any,
    b_sign_any,
    orb_any,
    addr_any,
    sign_any,
    seg_a_any,
    seg_b_any,
    allowed_any,
    out_ref,
    hot_ref,
    mask_ref,
    b_addr_ref,
    b_sign_ref,
    block_ref,
    orb_ref,
    addr_ref,
    sign_ref,
    seg_a_ref,
    seg_b_ref,
    allowed_ref,
    half_ref,
    turn_ref,
    big_sem,
    small_sem,
    table_sem,
    *,
    sizes,
    half,
    stride,
):
    norb, nbas = orb_ref.shape
    groups = big_ref.shape[1] // PACK
    starts = [sum(sizes[:s]) for s in range(len(sizes))]
    first = head_ref.shape[1]

    def fetch(s):
        return [
            pltpu.make_async_copy(
                big_ref.at[pl.ds(part * half + starts[s], sizes[s])],
                block_ref.at[part, pl.ds(starts[s] - first, sizes[s])],
                big_sem.at[s, part],
            )
            for part in range(2)
        ]

    small = [
        pltpu.make_async_copy(a, b, small_sem.at[k])
        for k, (a, b) in enumerate(
            (
                (orb_any, orb_ref),
                (addr_any, addr_ref),
                (sign_any, sign_ref),
                (seg_a_any, seg_a_ref),
                (seg_b_any, seg_b_ref),
                (allowed_any, allowed_ref),
            )
        )
    ]
    for copy in small:
        copy.start()
    late = [
        pltpu.make_async_copy(b_addr_any, b_addr_ref, table_sem.at[0]),
        pltpu.make_async_copy(b_sign_any, b_sign_ref, table_sem.at[1]),
    ]
    for s in range(1, 1 + AHEAD):
        for copy in fetch(s):
            copy.start()
    small[0].wait()
    weights = orb_ref[...]
    for s, size in enumerate(sizes):
        if s == len(sizes) - 1:
            for copy in late:
                copy.start()
        source, begin = (block_ref, starts[s] - first) if s else (head_ref, 0)
        for copy in fetch(s) if s else ():
            copy.wait()
        if 0 < s < len(sizes) - AHEAD:
            for copy in fetch(s + AHEAD):
                copy.start()
        cuts = [0, size // 2, size]
        total = [None, None]
        for part in range(2):
            for group in range(groups):
                placed = placed_rows(weights, (part * groups + group) * 32, LANES)
                for k in range(2):
                    block = source[
                        part,
                        begin + cuts[k] : begin + cuts[k + 1],
                        group * PACK : (group + 1) * PACK,
                        :,
                    ].reshape(-1, nbas)
                    piece = lax.dot_general(block, placed, NT, preferred_element_type=jnp.float32)
                    total[k] = piece if total[k] is None else total[k] + piece
        for k in range(2):
            for row in range(cuts[k + 1] - cuts[k]):
                half_ref[pl.ds(starts[s] + cuts[k] + row, PACK, stride=stride), :] = total[k][
                    row * PACK : (row + 1) * PACK, :
                ]
        if s == PREPARE_AT:
            for copy in small[1:]:
                copy.wait()
            prepare(addr_ref, sign_ref, seg_a_ref, seg_b_ref, allowed_ref, hot_ref, mask_ref)
    both = jnp.concatenate(
        [placed_rows(weights[:, part * half : (part + 1) * half], 0, 32) for part in range(2)], axis=0
    )
    for r in range(PACK):
        right = half_ref[r * stride : r * stride + half, :].astype(jnp.bfloat16)
        sums = jnp.dot(both, right, preferred_element_type=jnp.float32)
        turn_ref[pl.ds(r, norb, stride=PACK), :] = sums[:norb] + pltpu.roll(sums[32 : 32 + norb], LANES - groups * 32, 1)
    flatten(turn_ref, out_ref, norb, groups)
    for copy in late:
        copy.wait()


def flatten(turn_ref, out_ref, norb, groups):
    lane = lax.broadcasted_iota(jnp.int32, (PACK, LANES), 1)
    pairs = norb * norb
    tiles = -(-(pairs + (groups - 1) * 32) // LANES)
    value = [[jnp.zeros((PACK, LANES), jnp.float32) for _ in range(tiles)] for _ in range(groups)]
    for i in range(norb):
        moved = pltpu.roll(turn_ref[i * PACK : (i + 1) * PACK, :], i * norb % LANES, 1)
        for group in range(groups):
            begin = i * norb + group * 32
            for tile in range(begin // LANES, (begin + norb - 1) // LANES + 1):
                low = begin - tile * LANES
                keep = (lane >= low) & (lane < low + norb)
                value[group][tile] = jnp.where(keep, moved, value[group][tile])
    for group in range(groups):
        shift = group * 32
        for tile in range(-(-pairs // LANES)):
            ends = min(LANES, pairs - tile * LANES)
            result = value[group][tile]
            if shift:
                result = pltpu.roll(result, LANES - shift, 1)
                if tile + 1 < tiles:
                    result = jnp.where(
                        lane < LANES - shift, result, pltpu.roll(value[group][tile + 1], LANES - shift, 1)
                    )
            out_ref[group * PACK : (group + 1) * PACK, tile * LANES : tile * LANES + ends] = result[:, :ends].astype(
                jnp.bfloat16
            )


def transform(integrals, head, orbitals, tables, hot_shape, mask_shape, beta):
    aux, nbas, _ = integrals.shape
    norb = orbitals.shape[0]
    half = nbas // 2
    made = (jax.ShapeDtypeStruct(hot_shape, jnp.bfloat16), jax.ShapeDtypeStruct(mask_shape, jnp.float32))
    if head is None:
        half_done = jnp.einsum("jn,pmn->pjm", orbitals, integrals, preferred_element_type=jnp.float32).astype(
            jnp.bfloat16
        )
        factors = (
            jnp.einsum("im,pjm->pij", orbitals, half_done, preferred_element_type=jnp.float32)
            .reshape(aux, norb * norb)
            .astype(jnp.bfloat16)
        )
        return factors, *pl.pallas_call(prepare, out_shape=made, name="prepare")(*tables), *beta
    sizes = (head.shape[1],) + block_sizes(half - head.shape[1])
    stride = -(-half // 4) * 4
    stride += 4 if stride % SUBLANES == 0 else 0
    hbm = pl.BlockSpec(memory_space=pltpu.HBM)
    turned = jnp.transpose(integrals, (1, 0, 2))
    turned, orbitals, *tables = (
        pltpu.with_memory_space_constraint(t, pltpu.HBM) for t in (turned, orbitals, *tables)
    )
    beta = [pltpu.with_memory_space_constraint(t, pltpu.HBM) for t in beta]
    return pl.pallas_call(
        functools.partial(transform_kernel, sizes=sizes, half=half, stride=stride),
        in_specs=[hbm, pl.BlockSpec(memory_space=pltpu.VMEM)] + [hbm] * (3 + len(tables)),
        out_shape=(jax.ShapeDtypeStruct((aux, norb * norb), jnp.bfloat16),)
        + made
        + tuple(jax.ShapeDtypeStruct(t.shape, t.dtype) for t in beta),
        scratch_shapes=[
            pltpu.VMEM((2, half - sizes[0], aux, nbas), jnp.bfloat16),
            pltpu.VMEM(orbitals.shape, orbitals.dtype),
        ]
        + [pltpu.VMEM(t.shape, t.dtype) for t in tables]
        + [
            pltpu.VMEM((PACK * stride, LANES), jnp.float32),
            pltpu.VMEM((norb * PACK, LANES), jnp.float32),
            pltpu.SemaphoreType.DMA((len(sizes), 2)),
            pltpu.SemaphoreType.DMA((1 + len(tables),)),
            pltpu.SemaphoreType.DMA((2,)),
        ],
        cost_estimate=pl.CostEstimate(
            flops=4 * aux * nbas * nbas * LANES, transcendentals=0, bytes_accessed=2 * aux * nbas * nbas
        ),
        compiler_params=pltpu.CompilerParams(vmem_limit_bytes=WIDE_LIMIT),
        name="transform",
    )(turned, head, *beta, orbitals, *tables)


def block_sizes(rows):
    sizes, left = [], rows
    while left:
        size = min(left, BLOCK if left > BLOCK else BLOCK // 2)
        sizes.append(size)
        left -= size
    return tuple(sizes)


def split(value):
    high = value.astype(jnp.bfloat16)
    return high, (value - high.astype(jnp.float32)).astype(jnp.bfloat16)


def set_sources(vec_ref, mask_ref, source_ref):
    halves, mine, _ = mask_ref.shape
    held = source_ref.shape[1]
    core = lax.axis_index("grp") % halves
    for k in range(mine):
        source_ref[k // held, k % held : k % held + 1, :] = (
            vec_ref[core * mine + k].astype(jnp.float32) * mask_ref[core, k : k + 1, :]
        )


def gather_pairs(turn, addr_ref, sign_ref, source_ref, pairs_ref):
    pairs, n_beta = addr_ref.shape
    held = source_ref.shape[1]
    chunks = n_beta // LANES

    def gathered(k, index):
        value = None
        for c in range(chunks):
            row = jnp.broadcast_to(
                source_ref[turn, k : k + 1, c * LANES : (c + 1) * LANES], (index.shape[0], LANES)
            )
            found = jnp.take_along_axis(row, index % LANES if chunks > 1 else index, axis=1, mode="promise_in_bounds")
            value = found if value is None else jnp.where(index // LANES == c, found, value)
        return value

    def fill(start, count):
        for c in range(chunks):
            index = addr_ref[pl.ds(start, count), c * LANES : (c + 1) * LANES]
            sign = sign_ref[pl.ds(start, count), c * LANES : (c + 1) * LANES].astype(jnp.float32)
            for k in range(held):
                place = k * n_beta + c * LANES
                pairs_ref[pl.ds(start, count), place : place + LANES] = (gathered(k, index) * sign).astype(jnp.bfloat16)

    together = pairs // SUBLANES
    unroll = max(
        u for u in range(1, together + 1) if together % u == 0 and (u == 1 or u * held * chunks**2 <= UNROLL)
    )

    def step(i, carry):
        for u in range(unroll):
            fill(pl.multiple_of((i * unroll + u) * SUBLANES, SUBLANES), SUBLANES)
        return carry

    lax.fori_loop(0, together // unroll, step, 0)
    if pairs % SUBLANES:
        fill(together * SUBLANES, pairs % SUBLANES)


def set_alpha(factors, hot_ref, h_ref):
    side = hot_ref.shape[0]
    n_alpha, width = h_ref.shape
    total = None
    for q in range(side):
        part = lax.dot_general(
            hot_ref[q],
            placed_rows(factors, q * factors.shape[0], LANES),
            NT,
            preferred_element_type=jnp.float32,
        )
        total = part if total is None else total + part
    for g in range(width // LANES):
        h_ref[:, g * LANES : (g + 1) * LANES] = total[g * n_alpha : (g + 1) * n_alpha, :]


def contract_pairs(turn, factors, pairs_ref, t_ref, n_beta):
    aux, pairs = factors.shape
    held = t_ref.shape[1] // aux
    wide = max(1, 256 // n_beta)
    for first in range(0, held, wide):
        last = min(first + wide, held)
        part = jnp.dot(factors, pairs_ref[:pairs, first * n_beta : last * n_beta], preferred_element_type=jnp.float32)
        for k in range(first, last):
            t_ref[turn, k * aux : (k + 1) * aux, :] = part[:, (k - first) * n_beta : (k - first + 1) * n_beta]


def finish(h_ref, t_ref, mask_ref, turn_ref, out_ref):
    n_alpha, width = h_ref.shape
    n_beta = mask_ref.shape[2]
    h_high, h_low = split(h_ref[...])
    t_high, t_low = split(t_ref[...].reshape(width, n_beta))
    both = jnp.dot(jnp.concatenate([h_high, h_low], axis=0), t_high, preferred_element_type=jnp.float32)
    rest = jnp.dot(h_high, t_low, preferred_element_type=jnp.float32)
    partial = both[:n_alpha] + (both[n_alpha:] + rest)
    turn_ref[...] = (partial * mask_ref[...].reshape(n_alpha, n_beta)).T
    devices = out_ref.shape[0]
    local = n_beta // devices
    out_ref[...] = jnp.concatenate(
        [turn_ref[pl.ds(k, devices, stride=local), :] for k in range(local)], axis=1
    )


def gather_kernel(vec_ref, mask_ref, addr_ref, sign_ref, pairs_ref, source_ref):
    set_sources(vec_ref, mask_ref, source_ref)
    gather_pairs(0, addr_ref, sign_ref, source_ref, pairs_ref)


def contract_kernel(own_ref, other_ref, hot_ref, mask_ref, pairs_ref, out_ref, h_ref, t_ref, turn_ref):
    factors = jnp.concatenate([own_ref[...], other_ref[...]], axis=0)
    set_alpha(factors, hot_ref, h_ref)
    contract_pairs(0, factors, pairs_ref, t_ref, mask_ref.shape[2])
    finish(h_ref, t_ref, mask_ref, turn_ref, out_ref)


def beta_kernel(
    vec_ref,
    own_ref,
    other_ref,
    hot_ref,
    mask_ref,
    addr_ref,
    sign_ref,
    out_ref,
    source_ref,
    pairs_ref,
    h_ref,
    t_ref,
    turn_ref,
):
    set_sources(vec_ref, mask_ref, source_ref)
    factors = jnp.concatenate([own_ref[...], other_ref[...]], axis=0)
    set_alpha(factors, hot_ref, h_ref)

    @pl.loop(0, source_ref.shape[0])
    def _(turn):
        gather_pairs(turn, addr_ref, sign_ref, source_ref, pairs_ref)
        contract_pairs(turn, factors, pairs_ref, t_ref, mask_ref.shape[2])

    finish(h_ref, t_ref, mask_ref, turn_ref, out_ref)


def beta_side(vec, own, hot, mask, addr, sign, devices):
    aux, pairs = own.shape
    halves, mine, n_beta = mask.shape
    groups = lax.axis_size("grp")
    other = lax.ppermute(own, "grp", [(g, g ^ 1) for g in range(groups)])
    held = max(k for k in range(1, mine + 1) if mine % k == 0 and k * pairs * n_beta * 2 <= 12 * 2**20)
    params = pltpu.CompilerParams(vmem_limit_bytes=VMEM_LIMIT)
    made = jax.ShapeDtypeStruct((devices, n_beta // devices * halves * mine), jnp.float32)
    source = pltpu.VMEM((mine // held, held, n_beta), jnp.float32)
    product = jax.ShapeDtypeStruct((pairs, held * n_beta), jnp.bfloat16)
    sums = [
        pltpu.VMEM((halves * mine, mine * 2 * aux), jnp.float32),
        pltpu.VMEM((mine // held, held * 2 * aux, n_beta), jnp.float32),
        pltpu.VMEM((n_beta, halves * mine), jnp.float32),
    ]
    if held == mine:
        terms = pl.pallas_call(
            gather_kernel,
            out_shape=product,
            scratch_shapes=[source],
            compiler_params=params,
            cost_estimate=pl.CostEstimate(flops=0, transcendentals=0, bytes_accessed=8 * pairs * mine * n_beta),
            name="gather",
        )(vec, mask, addr, sign)
        return pl.pallas_call(
            contract_kernel, out_shape=made, scratch_shapes=sums, compiler_params=params, name="contract"
        )(own, other, hot, mask, terms)
    return pl.pallas_call(
        beta_kernel,
        out_shape=made,
        scratch_shapes=[source, pltpu.VMEM(product.shape, product.dtype)] + sums,
        compiler_params=params,
        name="beta_side",
    )(vec, own, other, hot, mask, addr, sign)


def add_kernel(parts_ref, out_ref):
    total = jnp.sum(parts_ref[...], axis=0, keepdims=True)
    rows, columns = out_ref.shape
    for k in range(rows):
        out_ref[k : k + 1, :] = total[:, k * columns : (k + 1) * columns]


def on_device(
    vector,
    integrals,
    orbitals,
    alpha_addr,
    alpha_sign,
    beta_addr,
    beta_sign,
    seg_alpha,
    seg_beta,
    allowed,
):
    devices = lax.axis_size(AXES)
    n_beta = vector.shape[1]
    n_alpha, pairs = alpha_addr.shape
    mine = n_alpha // 2
    side = LANES // (2 * integrals.shape[0])
    rows, head = start(vector, integrals, devices)
    vec = lax.all_to_all(
        rows, AXES, split_axis=0, concat_axis=0, tiled=True
    ).reshape(n_alpha, 1, n_beta)
    tables = (alpha_addr, alpha_sign, seg_alpha.reshape(1, -1), seg_beta.reshape(1, -1), allowed)
    own, hot, mask, addr, sign = transform(
        integrals, head, orbitals, tables, (side, mine // side * n_alpha, pairs), (2, mine, n_beta), (beta_addr.T, beta_sign.T)
    )
    partial = beta_side(vec, own, hot, mask, addr, sign, devices)
    parts = lax.all_to_all(partial, AXES, split_axis=0, concat_axis=0, tiled=True)
    return pl.pallas_call(
        add_kernel,
        out_shape=jax.ShapeDtypeStruct((n_beta // devices, n_alpha), jnp.float32),
        compiler_params=pltpu.CompilerParams(vmem_limit_bytes=VMEM_LIMIT),
        name="add_parts",
    )(parts)


def solution(mesh):
    rows = P(AXES, None)
    placed = (rows, P(AXES, None, None), P(), P(), P(), P(), P(), P(), P(), P())
    return jax.shard_map(on_device, mesh=mesh, in_specs=placed, out_specs=rows, check_vma=False)
```

```python
import functools

import jax
import jax.numpy as jnp
from jax import lax
from jax.experimental import pallas as pl
from jax.experimental.pallas import tpu as pltpu
from jax.sharding import PartitionSpec as P


AXES = ("grp", "blk")
LANES = 128
SUBLANES = 8
PACK = 16
UNROLL = 1344
AHEAD = 3
HEAD = 25
BLOCK = 50
PREPARE_AT = 2
VMEM_LIMIT = 32 * 2**20
WIDE_LIMIT = 50 * 2**20
NT = (((1,), (1,)), ((), ()))
TN = (((0,), (0,)), ((), ()))


def placed_rows(values, before, total):
    width = values.shape[1]
    pieces = [jnp.zeros((before, width), values.dtype)] if before else []
    pieces.append(values)
    after = total - before - values.shape[0]
    if after:
        pieces.append(jnp.zeros((after, width), values.dtype))
    return jnp.concatenate(pieces, axis=0) if len(pieces) > 1 else values


def prepare(addr_ref, sign_ref, seg_a_ref, seg_b_ref, allowed_ref, hot_ref, mask_ref):
    side, rows, _ = hot_ref.shape
    halves, held, n_beta = mask_ref.shape
    n_alpha = addr_ref.shape[0]
    blocks = allowed_ref.shape[0]
    base = lax.axis_index("grp") % halves * held
    addr = addr_ref[...] - base
    sign = sign_ref[...].astype(jnp.float32)
    for q in range(side):
        for g in range(rows // n_alpha):
            hot_ref[q, g * n_alpha : (g + 1) * n_alpha, :] = jnp.where(addr == g * side + q, sign, 0.0).astype(
                jnp.bfloat16
            )
    hot_b = (lax.broadcasted_iota(jnp.int32, (blocks, n_beta), 0) == seg_b_ref[...]).astype(jnp.float32)
    hot_a = (lax.broadcasted_iota(jnp.int32, (blocks, n_alpha), 0) == seg_a_ref[...]).astype(jnp.float32)
    columns = jnp.dot(allowed_ref[...].astype(jnp.float32), hot_b, preferred_element_type=jnp.float32)
    mask_ref[...] = lax.dot_general(hot_a, columns, TN, preferred_element_type=jnp.float32).reshape(
        halves, held, n_beta
    )


def start_kernel(vector_any, big_ref, out_any, head_ref, vector_ref, copy_ref, sem):
    size = head_ref.shape[1]
    vector = pltpu.make_async_copy(vector_any, vector_ref, sem.at[0])
    head = [
        pltpu.make_async_copy(
            big_ref.at[pl.ds(part * (big_ref.shape[0] // 2), size)], head_ref.at[part], sem.at[1 + part]
        )
        for part in range(2)
    ]
    out = pltpu.make_async_copy(copy_ref, out_any, sem.at[3])
    vector.start()
    for copy in head:
        copy.start()
    vector.wait()
    copy_ref[...] = jnp.broadcast_to(vector_ref[...][None], copy_ref.shape)
    out.start()
    out.wait()
    for copy in head:
        copy.wait()


def start(vector, integrals, devices):
    aux, nbas, _ = integrals.shape
    if not fits(integrals):
        return jnp.broadcast_to(vector, (devices,) + vector.shape), None
    hbm = pl.BlockSpec(memory_space=pltpu.HBM)
    vector, turned = (
        pltpu.with_memory_space_constraint(t, pltpu.HBM) for t in (vector, jnp.transpose(integrals, (1, 0, 2)))
    )
    return pl.pallas_call(
        start_kernel,
        in_specs=[hbm] * 2,
        out_specs=(hbm, pl.BlockSpec(memory_space=pltpu.VMEM)),
        out_shape=(
            jax.ShapeDtypeStruct((devices,) + vector.shape, vector.dtype),
            jax.ShapeDtypeStruct((2, min(HEAD, nbas // 2), aux, nbas), integrals.dtype),
        ),
        scratch_shapes=[
            pltpu.VMEM(vector.shape, vector.dtype),
            pltpu.VMEM((devices,) + vector.shape, vector.dtype),
            pltpu.SemaphoreType.DMA((4,)),
        ],
        compiler_params=pltpu.CompilerParams(vmem_limit_bytes=VMEM_LIMIT),
        name="start",
    )(vector, turned)


def fits(integrals):
    aux, nbas, _ = integrals.shape
    return aux % PACK == 0 and aux // PACK * 64 == LANES and nbas % 2 == 0


def transform_kernel(
    big_ref,
    head_ref,
    b_addr_any,
    b_sign_any,
    orb_any,
    addr_any,
    sign_any,
    seg_a_any,
    seg_b_any,
    allowed_any,
    out_ref,
    hot_ref,
    mask_ref,
    b_addr_ref,
    b_sign_ref,
    block_ref,
    orb_ref,
    addr_ref,
    sign_ref,
    seg_a_ref,
    seg_b_ref,
    allowed_ref,
    half_ref,
    turn_ref,
    big_sem,
    small_sem,
    table_sem,
    *,
    sizes,
    half,
    stride,
):
    norb, nbas = orb_ref.shape
    groups = big_ref.shape[1] // PACK
    starts = [sum(sizes[:s]) for s in range(len(sizes))]
    first = head_ref.shape[1]

    def fetch(s):
        return [
            pltpu.make_async_copy(
                big_ref.at[pl.ds(part * half + starts[s], sizes[s])],
                block_ref.at[part, pl.ds(starts[s] - first, sizes[s])],
                big_sem.at[s, part],
            )
            for part in range(2)
        ]

    small = [
        pltpu.make_async_copy(a, b, small_sem.at[k])
        for k, (a, b) in enumerate(
            (
                (orb_any, orb_ref),
                (addr_any, addr_ref),
                (sign_any, sign_ref),
                (seg_a_any, seg_a_ref),
                (seg_b_any, seg_b_ref),
                (allowed_any, allowed_ref),
            )
        )
    ]
    for copy in small:
        copy.start()
    late = [
        pltpu.make_async_copy(b_addr_any, b_addr_ref, table_sem.at[0]),
        pltpu.make_async_copy(b_sign_any, b_sign_ref, table_sem.at[1]),
    ]
    for s in range(1, 1 + AHEAD):
        for copy in fetch(s):
            copy.start()
    small[0].wait()
    weights = orb_ref[...]
    for s, size in enumerate(sizes):
        if s == len(sizes) - 1:
            for copy in late:
                copy.start()
        source, begin = (block_ref, starts[s] - first) if s else (head_ref, 0)
        for copy in fetch(s) if s else ():
            copy.wait()
        if 0 < s < len(sizes) - AHEAD:
            for copy in fetch(s + AHEAD):
                copy.start()
        cuts = [0, size // 2, size]
        total = [None, None]
        for part in range(2):
            for group in range(groups):
                placed = placed_rows(weights, (part * groups + group) * 32, LANES)
                for k in range(2):
                    block = source[
                        part,
                        begin + cuts[k] : begin + cuts[k + 1],
                        group * PACK : (group + 1) * PACK,
                        :,
                    ].reshape(-1, nbas)
                    piece = lax.dot_general(block, placed, NT, preferred_element_type=jnp.float32)
                    total[k] = piece if total[k] is None else total[k] + piece
        for k in range(2):
            for row in range(cuts[k + 1] - cuts[k]):
                half_ref[pl.ds(starts[s] + cuts[k] + row, PACK, stride=stride), :] = total[k][
                    row * PACK : (row + 1) * PACK, :
                ]
        if s == PREPARE_AT:
            for copy in small[1:]:
                copy.wait()
            prepare(addr_ref, sign_ref, seg_a_ref, seg_b_ref, allowed_ref, hot_ref, mask_ref)
    both = jnp.concatenate(
        [placed_rows(weights[:, part * half : (part + 1) * half], 0, 32) for part in range(2)], axis=0
    )
    for r in range(PACK):
        right = half_ref[r * stride : r * stride + half, :].astype(jnp.bfloat16)
        sums = jnp.dot(both, right, preferred_element_type=jnp.float32)
        turn_ref[pl.ds(r, norb, stride=PACK), :] = sums[:norb] + pltpu.roll(sums[32 : 32 + norb], LANES - groups * 32, 1)
    flatten(turn_ref, out_ref, norb, groups)
    for copy in late:
        copy.wait()


def flatten(turn_ref, out_ref, norb, groups):
    lane = lax.broadcasted_iota(jnp.int32, (PACK, LANES), 1)
    pairs = norb * norb
    tiles = -(-(pairs + (groups - 1) * 32) // LANES)
    value = [[jnp.zeros((PACK, LANES), jnp.float32) for _ in range(tiles)] for _ in range(groups)]
    for i in range(norb):
        moved = pltpu.roll(turn_ref[i * PACK : (i + 1) * PACK, :], i * norb % LANES, 1)
        for group in range(groups):
            begin = i * norb + group * 32
            for tile in range(begin // LANES, (begin + norb - 1) // LANES + 1):
                low = begin - tile * LANES
                keep = (lane >= low) & (lane < low + norb)
                value[group][tile] = jnp.where(keep, moved, value[group][tile])
    for group in range(groups):
        shift = group * 32
        for tile in range(-(-pairs // LANES)):
            ends = min(LANES, pairs - tile * LANES)
            result = value[group][tile]
            if shift:
                result = pltpu.roll(result, LANES - shift, 1)
                if tile + 1 < tiles:
                    result = jnp.where(
                        lane < LANES - shift, result, pltpu.roll(value[group][tile + 1], LANES - shift, 1)
                    )
            out_ref[group * PACK : (group + 1) * PACK, tile * LANES : tile * LANES + ends] = result[:, :ends].astype(
                jnp.bfloat16
            )


def transform(integrals, head, orbitals, tables, hot_shape, mask_shape, beta):
    aux, nbas, _ = integrals.shape
    norb = orbitals.shape[0]
    half = nbas // 2
    made = (jax.ShapeDtypeStruct(hot_shape, jnp.bfloat16), jax.ShapeDtypeStruct(mask_shape, jnp.float32))
    if head is None:
        half_done = jnp.einsum("jn,pmn->pjm", orbitals, integrals, preferred_element_type=jnp.float32).astype(
            jnp.bfloat16
        )
        factors = (
            jnp.einsum("im,pjm->pij", orbitals, half_done, preferred_element_type=jnp.float32)
            .reshape(aux, norb * norb)
            .astype(jnp.bfloat16)
        )
        return factors, *pl.pallas_call(prepare, out_shape=made, name="prepare")(*tables), *beta
    sizes = (head.shape[1],) + block_sizes(half - head.shape[1])
    stride = -(-half // 4) * 4
    stride += 4 if stride % SUBLANES == 0 else 0
    hbm = pl.BlockSpec(memory_space=pltpu.HBM)
    turned = jnp.transpose(integrals, (1, 0, 2))
    turned, orbitals, *tables = (
        pltpu.with_memory_space_constraint(t, pltpu.HBM) for t in (turned, orbitals, *tables)
    )
    beta = [pltpu.with_memory_space_constraint(t, pltpu.HBM) for t in beta]
    return pl.pallas_call(
        functools.partial(transform_kernel, sizes=sizes, half=half, stride=stride),
        in_specs=[hbm, pl.BlockSpec(memory_space=pltpu.VMEM)] + [hbm] * (3 + len(tables)),
        out_shape=(jax.ShapeDtypeStruct((aux, norb * norb), jnp.bfloat16),)
        + made
        + tuple(jax.ShapeDtypeStruct(t.shape, t.dtype) for t in beta),
        scratch_shapes=[
            pltpu.VMEM((2, half - sizes[0], aux, nbas), jnp.bfloat16),
            pltpu.VMEM(orbitals.shape, orbitals.dtype),
        ]
        + [pltpu.VMEM(t.shape, t.dtype) for t in tables]
        + [
            pltpu.VMEM((PACK * stride + SUBLANES, LANES), jnp.float32),
            pltpu.VMEM((-(-norb // SUBLANES) * SUBLANES * PACK, LANES), jnp.float32),
            pltpu.SemaphoreType.DMA((len(sizes), 2)),
            pltpu.SemaphoreType.DMA((1 + len(tables),)),
            pltpu.SemaphoreType.DMA((2,)),
        ],
        cost_estimate=pl.CostEstimate(
            flops=4 * aux * nbas * nbas * LANES, transcendentals=0, bytes_accessed=2 * aux * nbas * nbas
        ),
        compiler_params=pltpu.CompilerParams(vmem_limit_bytes=WIDE_LIMIT),
        name="transform",
    )(turned, head, *beta, orbitals, *tables)


def block_sizes(rows):
    sizes, left = [], rows
    while left:
        size = min(left, BLOCK if left > BLOCK else BLOCK // 2)
        sizes.append(size)
        left -= size
    return tuple(sizes)


def split(value):
    high = value.astype(jnp.bfloat16)
    return high, (value - high.astype(jnp.float32)).astype(jnp.bfloat16)


def set_sources(vec_ref, mask_ref, source_ref):
    halves, mine, _ = mask_ref.shape
    held = source_ref.shape[1]
    core = lax.axis_index("grp") % halves
    for k in range(mine):
        source_ref[k // held, k % held : k % held + 1, :] = (
            vec_ref[core * mine + k].astype(jnp.float32) * mask_ref[core, k : k + 1, :]
        )


def gather_pairs(turn, addr_ref, sign_ref, source_ref, pairs_ref):
    pairs, n_beta = addr_ref.shape
    held = source_ref.shape[1]
    chunks = n_beta // LANES

    def gathered(k, index):
        value = None
        for c in range(chunks):
            row = jnp.broadcast_to(
                source_ref[turn, k : k + 1, c * LANES : (c + 1) * LANES], (index.shape[0], LANES)
            )
            found = jnp.take_along_axis(row, index % LANES if chunks > 1 else index, axis=1, mode="promise_in_bounds")
            value = found if value is None else jnp.where(index // LANES == c, found, value)
        return value

    def fill(start, count):
        for c in range(chunks):
            index = addr_ref[pl.ds(start, count), c * LANES : (c + 1) * LANES]
            sign = sign_ref[pl.ds(start, count), c * LANES : (c + 1) * LANES].astype(jnp.float32)
            for k in range(held):
                place = k * n_beta + c * LANES
                pairs_ref[pl.ds(start, count), place : place + LANES] = (gathered(k, index) * sign).astype(jnp.bfloat16)

    together = pairs // SUBLANES
    unroll = max(
        u for u in range(1, together + 1) if together % u == 0 and (u == 1 or u * held * chunks**2 <= UNROLL)
    )

    def step(i, carry):
        for u in range(unroll):
            fill(pl.multiple_of((i * unroll + u) * SUBLANES, SUBLANES), SUBLANES)
        return carry

    lax.fori_loop(0, together // unroll, step, 0)
    if pairs % SUBLANES:
        fill(together * SUBLANES, pairs % SUBLANES)


def set_alpha(factors, hot_ref, h_ref):
    side = hot_ref.shape[0]
    n_alpha, width = h_ref.shape
    total = None
    for q in range(side):
        part = lax.dot_general(
            hot_ref[q],
            placed_rows(factors, q * factors.shape[0], LANES),
            NT,
            preferred_element_type=jnp.float32,
        )
        total = part if total is None else total + part
    for g in range(width // LANES):
        h_ref[:, g * LANES : (g + 1) * LANES] = total[g * n_alpha : (g + 1) * n_alpha, :]


def contract_pairs(turn, factors, pairs_ref, t_ref, n_beta):
    aux, pairs = factors.shape
    held = t_ref.shape[1] // aux
    wide = max(1, 256 // n_beta)
    for first in range(0, held, wide):
        last = min(first + wide, held)
        part = jnp.dot(factors, pairs_ref[:pairs, first * n_beta : last * n_beta], preferred_element_type=jnp.float32)
        for k in range(first, last):
            t_ref[turn, k * aux : (k + 1) * aux, :] = part[:, (k - first) * n_beta : (k - first + 1) * n_beta]


def finish(h_ref, t_ref, mask_ref, turn_ref, out_ref):
    n_alpha, width = h_ref.shape
    n_beta = mask_ref.shape[2]
    h_high, h_low = split(h_ref[...])
    t_high, t_low = split(t_ref[...].reshape(width, n_beta))
    both = jnp.dot(jnp.concatenate([h_high, h_low], axis=0), t_high, preferred_element_type=jnp.float32)
    rest = jnp.dot(h_high, t_low, preferred_element_type=jnp.float32)
    partial = both[:n_alpha] + (both[n_alpha:] + rest)
    turn_ref[...] = (partial * mask_ref[...].reshape(n_alpha, n_beta)).T
    devices = out_ref.shape[0]
    local = n_beta // devices
    out_ref[...] = jnp.concatenate(
        [turn_ref[pl.ds(k, devices, stride=local), :] for k in range(local)], axis=1
    )


def gather_kernel(vec_ref, mask_ref, addr_ref, sign_ref, pairs_ref, source_ref):
    set_sources(vec_ref, mask_ref, source_ref)
    gather_pairs(0, addr_ref, sign_ref, source_ref, pairs_ref)


def contract_kernel(own_ref, other_ref, hot_ref, mask_ref, pairs_ref, out_ref, h_ref, t_ref, turn_ref):
    factors = jnp.concatenate([own_ref[...], other_ref[...]], axis=0)
    set_alpha(factors, hot_ref, h_ref)
    contract_pairs(0, factors, pairs_ref, t_ref, mask_ref.shape[2])
    finish(h_ref, t_ref, mask_ref, turn_ref, out_ref)


def beta_kernel(
    vec_ref,
    own_ref,
    other_ref,
    hot_ref,
    mask_ref,
    addr_ref,
    sign_ref,
    out_ref,
    source_ref,
    pairs_ref,
    h_ref,
    t_ref,
    turn_ref,
):
    set_sources(vec_ref, mask_ref, source_ref)
    factors = jnp.concatenate([own_ref[...], other_ref[...]], axis=0)
    set_alpha(factors, hot_ref, h_ref)

    @pl.loop(0, source_ref.shape[0])
    def _(turn):
        gather_pairs(turn, addr_ref, sign_ref, source_ref, pairs_ref)
        contract_pairs(turn, factors, pairs_ref, t_ref, mask_ref.shape[2])

    finish(h_ref, t_ref, mask_ref, turn_ref, out_ref)


def beta_side(vec, own, hot, mask, addr, sign, devices):
    aux, pairs = own.shape
    halves, mine, n_beta = mask.shape
    groups = lax.axis_size("grp")
    other = lax.ppermute(own, "grp", [(g, g ^ 1) for g in range(groups)])
    held = max(k for k in range(1, mine + 1) if mine % k == 0 and k * pairs * n_beta * 2 <= 12 * 2**20)
    params = pltpu.CompilerParams(vmem_limit_bytes=VMEM_LIMIT)
    made = jax.ShapeDtypeStruct((devices, n_beta // devices * halves * mine), jnp.float32)
    source = pltpu.VMEM((mine // held, held, n_beta), jnp.float32)
    product = jax.ShapeDtypeStruct((-(-pairs // PACK) * PACK, held * n_beta), jnp.bfloat16)
    sums = [
        pltpu.VMEM((halves * mine, mine * 2 * aux), jnp.float32),
        pltpu.VMEM((mine // held, held * 2 * aux, n_beta), jnp.float32),
        pltpu.VMEM((n_beta, halves * mine), jnp.float32),
    ]
    if held == mine:
        terms = pl.pallas_call(
            gather_kernel,
            out_shape=product,
            scratch_shapes=[source],
            compiler_params=params,
            cost_estimate=pl.CostEstimate(flops=0, transcendentals=0, bytes_accessed=8 * pairs * mine * n_beta),
            name="gather",
        )(vec, mask, addr, sign)
        return pl.pallas_call(
            contract_kernel, out_shape=made, scratch_shapes=sums, compiler_params=params, name="contract"
        )(own, other, hot, mask, terms)
    return pl.pallas_call(
        beta_kernel,
        out_shape=made,
        scratch_shapes=[source, pltpu.VMEM(product.shape, product.dtype)] + sums,
        compiler_params=params,
        name="beta_side",
    )(vec, own, other, hot, mask, addr, sign)


def add_kernel(parts_ref, out_ref):
    total = jnp.sum(parts_ref[...], axis=0, keepdims=True)
    rows, columns = out_ref.shape
    for k in range(rows):
        out_ref[k : k + 1, :] = total[:, k * columns : (k + 1) * columns]


def on_device(
    vector,
    integrals,
    orbitals,
    alpha_addr,
    alpha_sign,
    beta_addr,
    beta_sign,
    seg_alpha,
    seg_beta,
    allowed,
):
    devices = lax.axis_size(AXES)
    n_beta = vector.shape[1]
    n_alpha, pairs = alpha_addr.shape
    mine = n_alpha // 2
    side = LANES // (2 * integrals.shape[0])
    rows, head = start(vector, integrals, devices)
    vec = lax.all_to_all(
        rows, AXES, split_axis=0, concat_axis=0, tiled=True
    ).reshape(n_alpha, 1, n_beta)
    tables = (alpha_addr, alpha_sign, seg_alpha.reshape(1, -1), seg_beta.reshape(1, -1), allowed)
    own, hot, mask, addr, sign = transform(
        integrals, head, orbitals, tables, (side, mine // side * n_alpha, pairs), (2, mine, n_beta), (beta_addr.T, beta_sign.T)
    )
    partial = beta_side(vec, own, hot, mask, addr, sign, devices)
    parts = lax.all_to_all(partial, AXES, split_axis=0, concat_axis=0, tiled=True)
    return pl.pallas_call(
        add_kernel,
        out_shape=jax.ShapeDtypeStruct((n_beta // devices, n_alpha), jnp.float32),
        compiler_params=pltpu.CompilerParams(vmem_limit_bytes=VMEM_LIMIT),
        name="add_parts",
    )(parts)


def solution(mesh):
    rows = P(AXES, None)
    placed = (rows, P(AXES, None, None), P(), P(), P(), P(), P(), P(), P(), P())
    return jax.shard_map(on_device, mesh=mesh, in_specs=placed, out_specs=rows, check_vma=False)
```
